128 devices in a mesh: tiles: 64 (over x, y, z), rows: 2 (over core).
Axes of the slice: x: 4, y: 4, z: 4, core: 2. Of those that a mesh axis runs over, the one named last changes fastest.
Arguments:
- frames: bfloat16 [64, 2, 64, 128, 256], P('tiles', None, None, 'rows'), may hold values from -6 to 6
- feat_weight: bfloat16 [9, 128, 64], replicated, may hold values from -0.25 to 0.25
- feat_bias: float32 [128], replicated, may hold values from -3 to 3
- send_rows: int32 [64, 2, 3, 2, 32], P('tiles', 'rows'), may hold values from 0 to 64, as said below
- recv_slots: int32 [64, 2, 64, 2], P('tiles', 'rows'), may hold values from 0 to 191, as said below
- blend: float32 [64, 2, 64, 2], P('tiles', 'rows'), may hold values from 0.2 to 0.8
- corr_weight: bfloat16 [256, 81], replicated, may hold values from -0.625 to 0.625
- corr_bias: float32 [256], replicated, may hold values from -4 to 4
- mid_weight: bfloat16 [9, 192, 256], replicated, may hold values from -0.125 to 0.125
- mid_bias: float32 [192], replicated, may hold values from -3 to 3
- flow_weight: bfloat16 [2, 192], replicated, may hold values from -0.4375 to 0.4375
- flow_bias: float32 [2], replicated, may hold values from -4 to 4
Outputs:
- flow: float32 [64, 2, 64, 128], P('tiles', None, 'rows')
The draws below stay inside these ranges and needn't reach their ends.
Inputs may be any that keep to these rules, and one draw needn't show every extreme that they name: `send_rows`: the lists come from the intersections of a ground band with the bands of its own and the two neighbouring chips. Frame f's feature row y of a band is numbered f * 32 + y; 64 marks an empty slot. What one band sends to another is one contiguous run of rows of one frame, in order, from slot 0, followed by empty slots. `recv_slots`: the value is w * 32 + c: slot c of window w as in the reference program. Both entries of a ground row are slots c and c + 1 of the same window. Each frame's ground rows of a band split into two contiguous runs, each served by one sender; every band reads from 4 of its 6 windows, which ones drawn per band. In every band one sender fills all 32 of its slots.
All inputs are finite; a program needn't handle non-finite values.
Results may differ from the reference program's by a relative error of at most 0.0059.
Values may be sent and summed in bfloat16 or wider, within the bound.
A program may use at most 192 MiB of HBM per device.

```python
import jax
import jax.numpy as jnp
from jax import lax

CIN = 64
CH = 128
HID = 256
MID = 192
RADIUS = 4
DILATION = 2
ROWS_OUT = 32
WIDTH = 128
WIDTH_IN = 256
TILE_IN = 128
TILE_OUT = 64
CAP = 32
OFFSETS = 81
N_TILES = 64
N_ROWS = 2
DEVICES = 128


def routing(key):
    window_count = 3 * N_ROWS

    def one_band(band_key, forced):
        band_keys = jax.random.split(band_key, 4)
        full_order = jax.random.permutation(band_keys[0], window_count).astype(jnp.int32)
        long_first = jax.random.randint(band_keys[1], (), 0, 2, dtype=jnp.int32)
        long_index = (1 - long_first).astype(jnp.int32)
        last_pos = jnp.argmax(full_order == window_count - 1).astype(jnp.int32)
        swapped = full_order.at[last_pos].set(full_order[long_index])
        swapped = swapped.at[long_index].set(window_count - 1)
        zero_pos = jnp.argmax(swapped == 0).astype(jnp.int32)
        swapped = swapped.at[zero_pos].set(swapped[2])
        swapped = swapped.at[2].set(0)
        order = jnp.where(forced, swapped, full_order)[:4]
        first_cut = jnp.where(long_first == 1, ROWS_OUT - 1, 1).astype(jnp.int32)
        second_cut = jax.random.randint(band_keys[2], (), 1, ROWS_OUT, dtype=jnp.int32)
        run_starts = jnp.stack([jnp.int32(0), first_cut, jnp.int32(0), second_cut])
        run_lengths = jnp.stack([first_cut, ROWS_OUT - first_cut, second_cut, ROWS_OUT - second_cut]).astype(jnp.int32)
        chip_starts = jax.random.randint(band_keys[3], (4,), 0, ROWS_OUT - run_lengths, dtype=jnp.int32)
        ground_row = jnp.arange(2 * ROWS_OUT, dtype=jnp.int32)
        frame_of = ground_row // ROWS_OUT
        within = ground_row % ROWS_OUT
        cut_of = jnp.where(frame_of == 0, first_cut, second_cut)
        run_of = frame_of * 2 + (within >= cut_of).astype(jnp.int32)
        window_of = order[run_of]
        offset_of = within - run_starts[run_of]
        slot_pair = jnp.stack([window_of * CAP + offset_of, window_of * CAP + offset_of + 1], axis=-1)
        slot_range = jnp.arange(CAP, dtype=jnp.int32)[None, :]
        window_range = jnp.arange(window_count, dtype=jnp.int32)[:, None]
        table = jnp.full((window_count, CAP), 2 * ROWS_OUT, jnp.int32)
        for run_index in range(4):
            frame_base = run_index // 2 * ROWS_OUT
            hit = (window_range == order[run_index]) & (slot_range <= run_lengths[run_index])
            table = jnp.where(hit, frame_base + chip_starts[run_index] + slot_range, table)
        return (table, slot_pair)
    band_keys = jax.random.split(jax.random.fold_in(key, 11), DEVICES)
    chosen_band = jax.random.randint(jax.random.fold_in(key, 23), (), 0, DEVICES, dtype=jnp.int32)
    forced_flags = jnp.arange(DEVICES, dtype=jnp.int32) == chosen_band
    tables, slot_pairs = jax.vmap(one_band)(band_keys, forced_flags)
    tables = tables.reshape(N_TILES, N_ROWS, 3, N_ROWS, CAP)
    send_tile = jnp.arange(N_TILES, dtype=jnp.int32)[:, None, None, None]
    send_core = jnp.arange(N_ROWS, dtype=jnp.int32)[None, :, None, None]
    chip_step = jnp.arange(3, dtype=jnp.int32)[None, None, :, None]
    recv_core = jnp.arange(N_ROWS, dtype=jnp.int32)[None, None, None, :]
    recv_tile = (send_tile + chip_step - 1 + N_TILES) % N_TILES
    send_table = tables[recv_tile, recv_core, chip_step, send_core]
    return (send_table, slot_pairs)


def draw_send_rows(key, part):
    send_table, slot_pairs = routing(key)
    return send_table


def draw_recv_slots(key, part):
    send_table, slot_pairs = routing(key)
    return slot_pairs.reshape(N_TILES, N_ROWS, 2 * ROWS_OUT, 2)


def shard_levels(stream_key, shape, cuts, low, largest):
    def one(axis_at, blocks):
        heights = jax.random.uniform(jax.random.fold_in(jax.random.fold_in(stream_key, 6), axis_at), (blocks,), jnp.float32, low / len(cuts), largest / len(cuts))
        return jnp.repeat(jnp.exp(heights), shape[axis_at] // blocks).reshape((-1,) + (1,) * (len(shape) - axis_at - 1))

    gain = one(*cuts[0])
    for cut in cuts[1:]:
        gain = gain * one(*cut)
    return gain


def gaussian(key, shape, deviation, most, pieces=(), kind=jnp.bfloat16):
    level = shard_levels(key, shape, pieces, -0.22, 0.18) if pieces else 1.0
    entries = jax.random.normal(key, shape, jnp.float32) * deviation * level
    return jnp.minimum(jnp.maximum(entries, -most), most).astype(kind)


def setup_inputs(seed: int = 0) -> dict:
    key_list = jax.random.split(jax.random.key(seed), 13)
    frames = gaussian(key_list[0], (N_TILES, 2, CIN, TILE_IN, WIDTH_IN), 1.0, 6.0, ((0, 64), (3, 2)))
    feat_weight = gaussian(key_list[1], (9, CH, CIN), (9 * CIN) ** -0.5, 0.25)
    feat_bias = gaussian(key_list[2], (CH,), 0.5, 3.0, (), jnp.float32)
    send_rows = draw_send_rows(jax.random.fold_in(key_list[12], 71), 0)
    recv_slots = draw_recv_slots(jax.random.fold_in(key_list[12], 71), 0)
    blend = jnp.clip(0.2 + 0.6 * jax.random.uniform(key_list[5], (N_TILES, N_ROWS, 2 * ROWS_OUT, 2), jnp.float32) ** shard_levels(key_list[5], (N_TILES, N_ROWS, 2 * ROWS_OUT, 2), ((0, 64), (1, 2)), -0.2, 0.2), 0.2, 0.8)
    corr_weight = gaussian(key_list[6], (HID, OFFSETS), OFFSETS ** -0.5, 0.625)
    corr_bias = gaussian(key_list[7], (HID,), 1.0, 4.0, (), jnp.float32)
    mid_weight = gaussian(key_list[8], (9, MID, HID), (9 * HID) ** -0.5, 0.125)
    mid_bias = gaussian(key_list[9], (MID,), 0.5, 3.0, (), jnp.float32)
    flow_weight = gaussian(key_list[10], (2, MID), MID ** -0.5, 0.4375)
    flow_bias = gaussian(key_list[11], (2,), 1.0, 4.0, (), jnp.float32)
    return dict(frames=frames, feat_weight=feat_weight, feat_bias=feat_bias, send_rows=send_rows, recv_slots=recv_slots, blend=blend, corr_weight=corr_weight, corr_bias=corr_bias, mid_weight=mid_weight, mid_bias=mid_bias, flow_weight=flow_weight, flow_bias=flow_bias)


def chip_features(frame_pair, feat_weight, feat_bias):
    kernel = feat_weight.reshape(3, 3, feat_weight.shape[1], feat_weight.shape[2]).transpose(2, 3, 0, 1)
    summed = lax.conv_general_dilated(frame_pair, kernel, (2, 2), ((1, 0), (1, 0)), preferred_element_type=jnp.float32)
    features = jax.nn.relu(summed + feat_bias[None, :, None, None]).astype(jnp.bfloat16)
    split_rows = features.reshape(2, CH, N_ROWS, ROWS_OUT, WIDTH).transpose(2, 0, 3, 1, 4)
    return split_rows.reshape(N_ROWS, 2 * ROWS_OUT, CH, WIDTH)


def correlate(first_frame, second_wide):
    reach = RADIUS * DILATION
    row_count, channels, columns = first_frame.shape
    padded = jnp.pad(second_wide, ((0, 0), (0, 0), (reach, reach))).astype(jnp.float32)
    first_wide = first_frame.astype(jnp.float32)
    collected = []
    for step_row in range(-RADIUS, RADIUS + 1):
        start_row = reach + step_row * DILATION
        row_band = padded[start_row:start_row + row_count]
        shifted = jnp.stack([row_band[:, :, reach + step_col * DILATION:reach + step_col * DILATION + columns] for step_col in range(-RADIUS, RADIUS + 1)])
        collected.append(jnp.einsum("hcw,dhcw->dhw", first_wide, shifted))
    return (jnp.concatenate(collected, axis=0) * channels ** -0.5).astype(jnp.bfloat16)


def tile_head(ground_pair, corr_weight, corr_bias, mid_weight, mid_bias, flow_weight, flow_bias):
    reach = RADIUS * DILATION
    second_wide = jnp.pad(ground_pair[1], ((reach, reach), (0, 0), (0, 0)))
    correlation = correlate(ground_pair[0], second_wide)
    hidden = jnp.einsum("oi,ihw->how", corr_weight.astype(jnp.float32), correlation.astype(jnp.float32))
    hidden = jax.nn.relu(hidden + corr_bias[None, :, None]).astype(jnp.bfloat16)
    widened = jnp.pad(hidden, ((1, 1), (0, 0), (1, 1))).astype(jnp.float32)
    row_count = hidden.shape[0]
    columns = hidden.shape[2]
    summed = jnp.zeros((row_count, MID, columns), jnp.float32)
    for tap_row in range(3):
        for tap_col in range(3):
            window = widened[tap_row:tap_row + row_count, :, tap_col:tap_col + columns]
            summed = summed + jnp.einsum("oi,hiw->how", mid_weight[3 * tap_row + tap_col].astype(jnp.float32), window)
    middle = jax.nn.relu(summed + mid_bias[None, :, None]).astype(jnp.bfloat16)
    return jnp.einsum("oi,hiw->ohw", flow_weight.astype(jnp.float32), middle.astype(jnp.float32)) + flow_bias[:, None, None]


def reference(frames, feat_weight, feat_bias, send_rows, recv_slots, blend, corr_weight, corr_bias, mid_weight, mid_bias, flow_weight, flow_bias):
    row_table = lax.map(lambda frame_pair: chip_features(frame_pair, feat_weight, feat_bias), frames)
    row_table = row_table.reshape(DEVICES, 2 * ROWS_OUT, CH, WIDTH)
    row_table = jnp.concatenate([row_table, jnp.zeros((DEVICES, 1, CH, WIDTH), row_table.dtype)], axis=1)
    send_table = send_rows.astype(jnp.int32)
    flat_slots = recv_slots.reshape(DEVICES, 2 * ROWS_OUT, 2).astype(jnp.int32)
    flat_blend = blend.reshape(DEVICES, 2 * ROWS_OUT, 2)

    def assemble(item):
        target, slot_values, weights = item
        tile_index = target // N_ROWS
        core_index = target % N_ROWS
        window_index = slot_values // CAP
        positions = slot_values % CAP
        chip_step = window_index // N_ROWS
        source_core = window_index % N_ROWS
        source_tile = (tile_index - chip_step + 1 + N_TILES) % N_TILES
        chosen = send_table[source_tile, source_core, chip_step, core_index, positions].astype(jnp.int32)
        picked = row_table[(source_tile * N_ROWS + source_core).astype(jnp.int32), chosen].astype(jnp.float32)
        return jnp.sum(weights[:, :, None, None] * picked, axis=1).astype(jnp.bfloat16)

    ground = lax.map(assemble, (jnp.arange(DEVICES, dtype=jnp.int32), flat_slots, flat_blend))
    ground = ground.reshape(N_TILES, N_ROWS, 2, ROWS_OUT, CH, WIDTH).transpose(0, 2, 1, 3, 4, 5)
    ground = ground.reshape(N_TILES, 2, TILE_OUT, CH, WIDTH)
    return lax.map(lambda ground_pair: tile_head(ground_pair, corr_weight, corr_bias, mid_weight, mid_bias, flow_weight, flow_bias), ground)
```

```python
import functools

import jax
import jax.numpy as jnp
import numpy as np
from jax import lax
from jax.experimental import pallas as pl
from jax.experimental.pallas import tpu as pltpu
from jax.sharding import PartitionSpec as P

BF16 = jnp.bfloat16
F32 = jnp.float32
MESH = pl.DeviceIdType.MESH

CIN = 64
CH = 128
HID = 256
MID = 192
WIDTH = 128
BAND = 32
GROUP = 8
CHUNKS = 2 * BAND // GROUP
SPAN = 9
NT = (((1,), (1,)), ((), ()))


def lane_of(offset):
    step_row, step_col = offset // SPAN, offset % SPAN
    return WIDTH * (step_row // 5) + 24 * (step_row % 5) + 7 + 2 * step_col


def column_picks():
    picks = np.zeros((2 * WIDTH, 3 * WIDTH), np.float32)
    for tap in range(3):
        for column in range(WIDTH):
            source = 2 * column - 1 + tap
            if source >= 0:
                picks[source, tap * WIDTH + column] = 1.0
    return picks


def offset_lanes():
    lanes = np.zeros((2 * WIDTH, SPAN * SPAN), np.float32)
    for offset in range(SPAN * SPAN):
        lanes[lane_of(offset), offset] = 1.0
    return lanes


def kernel(
    tiles,
    frames,
    picks,
    conv_w,
    feat_b,
    sent,
    slots,
    blend,
    lanes,
    corr_w,
    corr_b,
    mid_w,
    mid_b,
    flow_w,
    flow_b,
    out,
    xin,
    split,
    taps,
    bias_t,
    rows,
    table_v,
    table_s,
    g0,
    g1,
    keep,
    corr_k,
    hid,
    in_sem,
    halo_send,
    halo_recv,
    row_send,
    row_recv,
    table_send,
    table_recv,
    edge_send,
    edge_recv,
    local_sem,
):
    t = lax.axis_index("tiles")
    r = lax.axis_index("rows")
    right, left = lax.rem(t + 1, tiles), lax.rem(t + tiles - 1, tiles)
    other = 1 - r

    order = [(f, g) for f in range(2) for g in (3, 2, 1, 0)]
    loads = {}
    for f, g in order:
        loads[f, g] = pltpu.make_async_copy(
            frames.at[0, f, :, pl.ds(16 * g, 16), :], xin.at[f, g], in_sem.at[4 * f + g]
        )
        loads[f, g].start()

    peers = [(right, r), (left, r), (t, other), (right, other), (left, other)]
    barrier = pltpu.get_barrier_semaphore()
    for peer in peers:
        pl.semaphore_signal(barrier, inc=1, device_id=peer, device_id_type=MESH)

    bias_t[...] = jnp.broadcast_to(feat_b[...], (CH, CH)).T
    taps[:, 0] = jnp.zeros((2, 3 * CIN, WIDTH), BF16)

    def split_group(f, g):
        loads[f, g].wait()

        def columns(i, carry):
            part = xin[f, g, pl.ds(16 * i, 16)].reshape(256, 2 * WIDTH)
            found = jnp.dot(part, picks[...], preferred_element_type=F32)
            for b in range(3):
                split[b, pl.ds(256 * i, 256), :] = found[:, b * WIDTH : (b + 1) * WIDTH]
            return carry

        lax.fori_loop(0, 4, columns, 0)

        def regroup(i, carry):
            for b in range(3):
                taps[f, 1 + 16 * g + i, b * CIN : (b + 1) * CIN, :] = split[
                    b, pl.ds(i, CIN, stride=16), :
                ].astype(BF16)
            return carry

        lax.fori_loop(0, 16, regroup, 0, unroll=4)

    def conv_group(f, g):
        def pair(p, carry):
            y = 8 * g + 2 * p
            upper = taps[f, pl.ds(2 * y, 3)].reshape(9 * CIN, WIDTH)
            lower = taps[f, pl.ds(2 * y + 2, 3)].reshape(9 * CIN, WIDTH)
            found = jnp.dot(
                conv_w[...],
                jnp.concatenate([upper, lower], axis=1),
                preferred_element_type=F32,
            )
            for i in range(2):
                feature = found[:, i * WIDTH : (i + 1) * WIDTH] + bias_t[...]
                rows[2 + r, f * BAND + y + i] = jnp.maximum(feature, 0.0).astype(BF16).T
            return carry

        lax.fori_loop(0, 4, pair, 0)

    def remote(src, dst, send, recv, peer):
        return pltpu.make_async_remote_copy(
            src_ref=src, dst_ref=dst, send_sem=send, recv_sem=recv, device_id=peer, device_id_type=MESH
        )

    def row_copy(kind, j):
        window = (2 * (2, 0, 1, 2, 0)[kind]) + r
        place = (1, 1, 1, 2, 0)[kind] * 2 + r
        peer = ((right, r), (left, r), (t, other), (t, other), (t, other))[kind]
        part = pl.ds(GROUP * j, GROUP)
        return remote(
            rows.at[place, part],
            rows.at[window, part],
            row_send.at[kind, j],
            row_recv.at[kind, j],
            peer,
        )

    table_v[2 + r] = sent[0, 0]
    halos = [
        remote(taps.at[f, 64], taps.at[f, 65], halo_send.at[f], halo_recv.at[f], (t, other))
        for f in range(2)
    ]
    tables = []
    for i, peer in enumerate(peers):
        window = (4, 0, 2, 4, 0)[i] + r
        tables.append(remote(table_v.at[2 + r], table_v.at[window], table_send.at[i], table_recv.at[i], peer))

    split_group(0, 3)
    pl.semaphore_wait(barrier, 5)
    for copy in tables:
        copy.start()
    for f in range(2):
        if f:
            split_group(f, 3)
        halos[f].start()
        for g in (3, 2, 1, 0):
            if g:
                split_group(f, g - 1)
            else:
                halos[f].wait()
                above = taps[f, 65]
                taps[f, 0] = jnp.where(r == 0, jnp.zeros_like(above), above)
            conv_group(f, g)
            for kind in range(3):
                row_copy(kind, 4 * f + g).start()

    keep_lane = lax.broadcasted_iota(jnp.int32, (WIDTH, WIDTH), 1)
    keep_x = WIDTH - 1 - lax.broadcasted_iota(jnp.int32, (WIDTH, WIDTH), 0)
    mirror = jnp.where(keep_lane == keep_x, 1.0, 0.0)
    for u in range(SPAN):
        step = keep_lane - lane_of(SPAN * u) % WIDTH
        target = keep_x + step - 8
        valid = (step >= 0) & (step <= 16) & (step % 2 == 0) & (target >= 0) & (target < WIDTH)
        keep[u] = jnp.where(valid, 1.0, 0.0)
    corr_k[...] = lax.dot_general(lanes[...], corr_w[...], NT, preferred_element_type=F32).astype(BF16)
    g1[pl.ds(41 * r, 8)] = jnp.zeros((8, WIDTH, CH), BF16)
    hid[33 * r] = jnp.zeros((WIDTH, 3 * HID), BF16)

    for copy in tables:
        copy.wait()
    to_scalar = pltpu.make_async_copy(table_v, table_s, local_sem)
    to_scalar.start()

    chunk_order = [4 * f + g for f in range(2) for g in (3, 2, 1, 0)]
    for j in chunk_order:
        for kind in range(2):
            row_copy(kind, j).wait_recv()
            row_copy(3 + kind, j).start()
    to_scalar.wait()
    for j in chunk_order:
        for kind in (2, 3, 4):
            row_copy(kind, j).wait_recv()

    def source(j, i):
        slot = slots[0, 0, j, i]
        window = slot // BAND
        row = table_s[window, window // 2, r, slot % BAND]
        weight = jnp.where(row < 2 * BAND, blend[0, 0, j, i], 0.0)
        return weight * rows[window, jnp.minimum(row, 2 * BAND - 1)].astype(F32)

    def ground(y, carry):
        g1[8 + r + y] = (source(BAND + y, 0) + source(BAND + y, 1)).astype(BF16)
        first = (source(y, 0) + source(y, 1)).astype(BF16)
        g0[r + y] = jnp.dot(mirror.astype(BF16), first, preferred_element_type=F32).astype(BF16)
        return carry

    lax.fori_loop(0, BAND, ground, 0)

    edges = [
        remote(
            g1.at[pl.ds(31 - 22 * r, 9)], g1.at[pl.ds(40 * r, 9)], edge_send.at[0], edge_recv.at[0], (t, other)
        ),
        remote(g0.at[31 - 30 * r], g0.at[32 * r], edge_send.at[1], edge_recv.at[1], (t, other)),
    ]
    for copy in edges:
        copy.start()
    for copy in edges:
        copy.wait()

    side = lax.broadcasted_iota(jnp.int32, (WIDTH, HID), 0)

    def hidden(h, carry):
        first = g0[h]
        packed = [jnp.zeros((WIDTH, WIDTH), F32)] * 2
        for u in range(SPAN):
            found = lax.dot_general(first, g1[h + 2 * u], NT, preferred_element_type=F32)
            turned = jnp.concatenate(
                [
                    pltpu.roll(
                        found[k : k + 8], (lane_of(SPAN * u) + 9 + k) % WIDTH, 1, stride=1, stride_axis=0
                    )
                    for k in range(0, WIDTH, 8)
                ],
                axis=0,
            )
            packed[u // 5] = jnp.where(keep[u] > 0.0, turned, packed[u // 5])
        value = jnp.dot((jnp.concatenate(packed, axis=1) * CH**-0.5).astype(BF16), corr_k[...], preferred_element_type=F32)
        value = jnp.maximum(value + corr_b[...], 0.0)
        before = jnp.where(side == 0, 0.0, pltpu.roll(value, 1, 0))
        after = jnp.where(side == WIDTH - 1, 0.0, pltpu.roll(value, WIDTH - 1, 0))
        at = h + 1 - r
        hid[at, :, 0:HID] = after.astype(BF16)
        hid[at, :, HID : 2 * HID] = value.astype(BF16)
        hid[at, :, 2 * HID : 3 * HID] = before.astype(BF16)
        return carry

    lax.fori_loop(0, BAND + 1, hidden, 0, unroll=3)

    def head(i, carry):
        y = 4 * i
        total = None
        for a in range(3):
            part = hid[pl.ds(y + a, 4)].reshape(4 * WIDTH, 3 * HID)
            term = jnp.dot(part, mid_w[a], preferred_element_type=F32)
            total = term if total is None else total + term
        middle = jnp.maximum(total + mid_b[...], 0.0).astype(BF16)
        flow = lax.dot_general(flow_w[...], middle, NT, preferred_element_type=F32)
        for c in range(2):
            for k in range(4):
                out[0, c, pl.ds(y + k, 1), :] = flow[c : c + 1, k * WIDTH : (k + 1) * WIDTH] + flow_b[c]
        return carry

    lax.fori_loop(0, BAND // 4, head, 0)
    for c in range(2):
        out[0, c] = jnp.dot(
            out[0, c], mirror, preferred_element_type=F32, precision=lax.Precision.HIGHEST
        )

    for j in chunk_order:
        for kind in range(5):
            row_copy(kind, j).wait_send()


def on_device(
    tiles,
    frames,
    feat_weight,
    feat_bias,
    send_rows,
    recv_slots,
    blend,
    corr_weight,
    corr_bias,
    mid_weight,
    mid_bias,
    flow_weight,
    flow_bias,
):
    conv_w = feat_weight.transpose(1, 0, 2).reshape(CH, 9 * CIN)
    mid_w = mid_weight.transpose(0, 2, 1).reshape(3, 3 * HID, MID)
    vmem = pl.BlockSpec(memory_space=pltpu.VMEM)
    smem = pl.BlockSpec(memory_space=pltpu.SMEM)
    dma = pltpu.SemaphoreType.DMA
    return pl.pallas_call(
        functools.partial(kernel, tiles),
        out_shape=jax.ShapeDtypeStruct((1, 2, BAND, WIDTH), F32),
        in_specs=[pl.BlockSpec(memory_space=pl.ANY)]
        + [vmem] * 4
        + [smem] * 2
        + [vmem] * 6
        + [smem],
        out_specs=vmem,
        scratch_shapes=[
            pltpu.VMEM((2, 4, CIN, 16, 2 * WIDTH), BF16),
            pltpu.VMEM((3, 16 * CIN, WIDTH), F32),
            pltpu.VMEM((2, 66, 3 * CIN, WIDTH), BF16),
            pltpu.VMEM((CH, CH), F32),
            pltpu.VMEM((6, 2 * BAND, WIDTH, CH), BF16),
            pltpu.VMEM((6, 3, 2, BAND), jnp.int32),
            pltpu.SMEM((6, 3, 2, BAND), jnp.int32),
            pltpu.VMEM((BAND + 1, WIDTH, CH), BF16),
            pltpu.VMEM((BAND + 17, WIDTH, CH), BF16),
            pltpu.VMEM((SPAN, WIDTH, WIDTH), F32),
            pltpu.VMEM((2 * WIDTH, HID), BF16),
            pltpu.VMEM((BAND + 2, WIDTH, 3 * HID), BF16),
            dma((8,)),
            dma((2,)),
            dma((2,)),
            dma((5, CHUNKS)),
            dma((5, CHUNKS)),
            dma((5,)),
            dma((5,)),
            dma((2,)),
            dma((2,)),
            dma,
        ],
        compiler_params=pltpu.CompilerParams(
            collective_id=0, has_side_effects=True, vmem_limit_bytes=56 * 1024 * 1024
        ),
    )(
        frames,
        jnp.asarray(column_picks(), BF16),
        conv_w,
        feat_bias.reshape(1, CH),
        send_rows,
        recv_slots,
        blend,
        jnp.asarray(offset_lanes(), BF16),
        corr_weight,
        corr_bias.reshape(1, HID),
        mid_w,
        mid_bias.reshape(1, MID),
        flow_weight,
        flow_bias,
    )


def solution(mesh):
    return jax.shard_map(
        functools.partial(on_device, mesh.shape["tiles"]),
        mesh=mesh,
        in_specs=(
            P("tiles", None, None, "rows", None),
            P(),
            P(),
            P("tiles", "rows", None, None, None),
            P("tiles", "rows", None, None),
            P("tiles", "rows", None, None),
            P(),
            P(),
            P(),
            P(),
            P(),
            P(),
        ),
        out_specs=P("tiles", None, "rows", None),
        check_vma=False,
    )
```

```python
import functools

import jax
import jax.numpy as jnp
import numpy as np
from jax import lax
from jax.experimental import pallas as pl
from jax.experimental.pallas import tpu as pltpu
from jax.sharding import PartitionSpec as P

BF16 = jnp.bfloat16
F32 = jnp.float32
MESH = pl.DeviceIdType.MESH

CIN = 64
CH = 128
HID = 256
MID = 192
WIDTH = 128
BAND = 32
GROUP = 8
GROUPS = 2 * BAND // GROUP
SPAN = 9
NT = (((1,), (1,)), ((), ()))
TN = (((0,), (0,)), ((), ()))

PARTS = (((0, 96), (0, 80), (0, 64)), ((96, 128), (80, 128), (64, 128)))


def centre_of(step_row):
    return 24 * (step_row % 5) + 15


def offset_lanes():
    lanes = np.zeros((2 * WIDTH, SPAN * SPAN), np.float32)
    for offset in range(SPAN * SPAN):
        step_row, step_col = offset // SPAN, offset % SPAN
        lanes[WIDTH * (step_row // 5) + centre_of(step_row) + 8 - 2 * step_col, offset] = 1.0
    return lanes


def kernel(
    tiles,
    frames,
    feat_w,
    feat_b,
    sent,
    slots,
    blend,
    lanes,
    corr_w,
    corr_b,
    mid_w,
    mid_b,
    flow_w,
    flow_b,
    out,
    xin,
    picks,
    conv_w,
    split,
    taps,
    bias_t,
    rows_0,
    rows_1,
    table_v,
    table_s,
    g0,
    g1,
    g1_t,
    halo,
    mirror,
    packed,
    corr_k,
    tail,
    hid,
    mid_in,
    mid_k,
    in_sem,
    halo_send,
    halo_recv,
    row_send,
    row_recv,
    table_send,
    table_recv,
    edge_send,
    edge_recv,
    local_sem,
):
    t = lax.axis_index("tiles")
    r = lax.axis_index("rows")
    right, left = lax.rem(t + 1, tiles), lax.rem(t + tiles - 1, tiles)
    other = 1 - r
    rows = (rows_0, rows_1)

    order = [(f, g) for f in range(2) for g in (3, 2, 1, 0)]
    loads = {}
    for f, g in order:
        loads[f, g] = pltpu.make_async_copy(
            frames.at[0, f, :, pl.ds(16 * g, 16), :], xin.at[f, g], in_sem.at[4 * f + g]
        )
        loads[f, g].start()
    mid_load = pltpu.make_async_copy(mid_w, mid_in, local_sem.at[0])
    mid_load.start()

    peers = [(right, r), (left, r), (t, other), (right, other), (left, other)]
    barrier = pltpu.get_barrier_semaphore()
    for peer in peers:
        pl.semaphore_signal(barrier, inc=1, device_id=peer, device_id_type=MESH)

    column = lax.broadcasted_iota(jnp.int32, (2 * WIDTH, WIDTH), 0)
    target = lax.broadcasted_iota(jnp.int32, (2 * WIDTH, WIDTH), 1)
    for b in range(3):
        picks[:, b * WIDTH : (b + 1) * WIDTH] = jnp.where(column == 2 * target - 1 + b, 1.0, 0.0).astype(BF16)
    conv_w[...] = feat_w[...].T
    bias_t[...] = jnp.broadcast_to(feat_b[...], (CH, CH)).T
    taps[:, 0] = jnp.zeros((2, 3 * CIN, WIDTH), BF16)

    def split_group(f, g):
        loads[f, g].wait()

        def columns(i, carry):
            part = xin[f, g, pl.ds(16 * i, 16)].reshape(256, 2 * WIDTH)
            found = jnp.dot(part, picks[...], preferred_element_type=F32)
            for b in range(3):
                split[b, pl.ds(256 * i, 256), :] = found[:, b * WIDTH : (b + 1) * WIDTH]
            return carry

        lax.fori_loop(0, 4, columns, 0)

        def regroup(i, carry):
            for b in range(3):
                taps[f, 1 + 16 * g + i, b * CIN : (b + 1) * CIN, :] = split[
                    b, pl.ds(i, CIN, stride=16), :
                ].astype(BF16)
            return carry

        lax.fori_loop(0, 16, regroup, 0, unroll=4)

    def conv_group(f, g):
        def pair(p, carry):
            y = 8 * g + 2 * p
            upper = taps[f, pl.ds(2 * y, 3)].reshape(9 * CIN, WIDTH)
            lower = taps[f, pl.ds(2 * y + 2, 3)].reshape(9 * CIN, WIDTH)
            found = jnp.dot(
                conv_w[...],
                jnp.concatenate([upper, lower], axis=1),
                preferred_element_type=F32,
            )
            for i in range(2):
                feature = found[:, i * WIDTH : (i + 1) * WIDTH] + bias_t[...]
                feature = jnp.maximum(feature, 0.0).astype(BF16).T
                for k in range(len(PARTS)):
                    low, high = PARTS[k][0]
                    rows[k][2 + r, f * BAND + y + i] = feature[low:high]
            return carry

        lax.fori_loop(0, 4, pair, 0)

    def remote(src, dst, send, recv, peer):
        return pltpu.make_async_remote_copy(
            src_ref=src, dst_ref=dst, send_sem=send, recv_sem=recv, device_id=peer, device_id_type=MESH
        )

    def row_copy(kind, k, j):
        window = 2 * (2, 0, 1, 2, 0)[kind] + r
        place = 2 * (1, 1, 1, 2, 0)[kind] + r
        peer = ((right, r), (left, r), (t, other), (t, other), (t, other))[kind]
        part = pl.ds(GROUP * j, GROUP)
        return remote(
            rows[k].at[place, part],
            rows[k].at[window, part],
            row_send.at[kind, k, j],
            row_recv.at[kind, k, j],
            peer,
        )

    table_v[2 + r] = sent[0, 0]
    halos = [
        remote(taps.at[f, 64], taps.at[f, 65], halo_send.at[f], halo_recv.at[f], (t, other))
        for f in range(2)
    ]
    tables = []
    for i, peer in enumerate(peers):
        window = (4, 0, 2, 4, 0)[i] + r
        tables.append(remote(table_v.at[2 + r], table_v.at[window], table_send.at[i], table_recv.at[i], peer))

    split_group(0, 3)
    pl.semaphore_wait(barrier, 5)
    for f in range(2):
        if f:
            split_group(f, 3)
        halos[f].start()
        for g in (3, 2, 1, 0):
            if g:
                split_group(f, g - 1)
            else:
                halos[f].wait()
                above = taps[f, 65]
                taps[f, 0] = jnp.where(r == 0, jnp.zeros_like(above), above)
            conv_group(f, g)
            for kind in range(3):
                row_copy(kind, 0, 4 * f + g).start()
        if f == 0:
            for copy in tables:
                copy.start()
    group_order = [4 * f + g for f, g in order]
    for k in range(1, len(PARTS)):
        for j in group_order:
            for kind in range(3):
                row_copy(kind, k, j).start()

    lane = lax.broadcasted_iota(jnp.int32, (WIDTH, WIDTH), 1)
    place = lax.broadcasted_iota(jnp.int32, (WIDTH, WIDTH), 0)
    mirror[...] = jnp.where(lane == WIDTH - 1 - place, 1.0, 0.0).astype(BF16)
    corr_k[...] = jnp.dot(lanes[...], corr_w[...], preferred_element_type=F32).astype(BF16)
    hid[33 * r] = jnp.zeros((WIDTH, 3 * HID), BF16)

    def clear(i, carry):
        packed[i] = jnp.zeros((WIDTH, 2 * WIDTH), F32)
        return carry

    lax.fori_loop(0, BAND, clear, 0)

    def clear_rim(i, carry):
        g1_t[i % 2 * 24 + 20 * r + i // 2] = jnp.zeros((CH, WIDTH), BF16)
        return carry

    lax.fori_loop(0, 8, clear_rim, 0)
    mid_load.wait()
    for tap in range(9):
        a, b = tap // 3, tap % 3
        mid_k[a, b * HID : (b + 1) * HID, :] = mid_in[tap].T

    for copy in tables:
        copy.wait()
    to_scalar = pltpu.make_async_copy(table_v, table_s, local_sem.at[1])
    to_scalar.start()
    to_scalar.wait()

    lane8 = lax.broadcasted_iota(jnp.int32, (8, WIDTH), 1)
    place8 = lax.broadcasted_iota(jnp.int32, (8, WIDTH), 0)

    def do_part(k):
        (a0, a1), (c0, c1), (m0, m1) = PARTS[k]
        width = c1 - c0

        for j in group_order:
            for kind in range(2):
                row_copy(kind, k, j).wait_recv()
                row_copy(3 + kind, k, j).start()
        for j in group_order:
            for kind in (2, 3, 4):
                row_copy(kind, k, j).wait_recv()

        def source(j, i):
            slot = slots[0, 0, i, j]
            window = slot // BAND
            row = table_s[window, window // 2, r, slot % BAND]
            weight = jnp.where(row < 2 * BAND, blend[0, 0, i, j], 0.0)
            return weight * rows[k][window, jnp.minimum(row, 2 * BAND - 1)].astype(F32)

        def turn(where, value):
            turned = lax.dot_general(value, mirror[a0:a1], TN, preferred_element_type=F32).astype(BF16)
            if k:
                turned = g1_t[where] + turned
            g1_t[where] = turned

        def ground(i, carry):
            y = lax.rem(24 * other + i, BAND)
            parity, half = lax.rem(y, 2), y // 2
            g0[16 * parity + half, a0:a1] = (source(y, 0) + source(y, 1)).astype(BF16)
            second = (source(BAND + y, 0) + source(BAND + y, 1)).astype(BF16)
            g1[y, a0:a1] = second
            turn(24 * parity + 4 + half, second)
            return carry

        lax.fori_loop(0, 8, ground, 0, unroll=2)
        edge = remote(
            g1.at[pl.ds(24 * other, 8), pl.ds(a0, a1 - a0)],
            halo.at[:, pl.ds(a0, a1 - a0)],
            edge_send.at[0, k],
            edge_recv.at[0, k],
            (t, other),
        )
        edge.start()
        lax.fori_loop(8, BAND, ground, 0, unroll=2)
        edge.wait()

        def ground_halo(i, carry):
            turn(24 * lax.rem(i, 2) + 20 * other + i // 2, halo[i, a0:a1])
            return carry

        lax.fori_loop(0, 8, ground_halo, 0, unroll=2)

        def correlate(b, carry):
            parity, block = lax.rem(b, 2), b // 2
            first = 16 * parity + 4 * block
            second = 24 * parity + 4 * block
            for j in range(0, 12, 2):
                low, high = max(0, j - 8), min(4, j + 2)
                left_side = g0[pl.ds(first + low, high - low), c0:c1].reshape((high - low) * width, CH)
                pair = jnp.concatenate([g1_t[second + j], g1_t[second + j + 1]], axis=1)
                found = jnp.dot(left_side, pair, preferred_element_type=F32)
                for h in range(low, high):
                    for e in range(2):
                        u = j + e - h
                        if not 0 <= u < SPAN:
                            continue
                        centre = centre_of(u)
                        for x in range(c0, c1, 8):
                            at = (h - low) * width + x - c0
                            turned = pltpu.roll(
                                found[at : at + 8, e * WIDTH : (e + 1) * WIDTH],
                                (centre + 1 + x) % WIDTH,
                                1,
                                stride=1,
                                stride_axis=0,
                            )
                            mask = (lane8 >= centre - 8) & (lane8 <= centre + 8)
                            if x == 0:
                                mask = mask & (place8 + centre - lane8 >= 0)
                            if x == WIDTH - 8:
                                mask = mask & (place8 + centre - lane8 < 8)
                            pltpu.store(
                                packed.at[
                                    first + h, pl.ds(x, 8), pl.ds(WIDTH * (u // 5), WIDTH)
                                ],
                                turned,
                                mask=mask,
                            )
            return carry

        lax.fori_loop(0, 8, correlate, 0)

        kept = 16 if k else 0
        side = lax.broadcasted_iota(jnp.int32, (width + kept, HID), 0)

        def hidden(i, carry):
            at = 2 * lax.rem(i, 16) + i // 16 + 1
            scaled = (packed[i, c0:c1] * CH**-0.5).astype(BF16)
            value = jnp.dot(scaled, corr_k[...], preferred_element_type=F32)
            value = jnp.maximum(value + corr_b[...], 0.0)
            whole = jnp.concatenate([tail[i], value], axis=0) if k else value
            before = pltpu.roll(whole, 1, 0)
            after = pltpu.roll(whole, width + kept - 1, 0)
            if k == 0:
                before = jnp.where(side == 0, 0.0, before)
            if k == len(PARTS) - 1:
                after = jnp.where(side == width + kept - 1, 0.0, after)
            else:
                tail[i] = value[width - 16 :]
            hid[at, c0:c1, 0:HID] = before[kept:].astype(BF16)
            hid[at, c0:c1, HID : 2 * HID] = value.astype(BF16)
            hid[at, m0:m1, 2 * HID : 3 * HID] = after[0 : m1 - m0].astype(BF16)
            return carry

        lax.fori_loop(0, BAND, hidden, 0, unroll=4)

        rim = remote(
            hid.at[32 - 31 * r, pl.ds(m0, m1 - m0)],
            hid.at[33 * r, pl.ds(m0, m1 - m0)],
            edge_send.at[1, k],
            edge_recv.at[1, k],
            (t, other),
        )
        rim_in = remote(
            hid.at[32 - 31 * r, pl.ds(m0, m1 - m0)],
            hid.at[33 * other, pl.ds(m0, m1 - m0)],
            edge_send.at[1, k],
            edge_recv.at[1, k],
            (t, other),
        )
        rim.start()
        columns = m1 - m0

        def head(i, carry):
            y = 8 * lax.rem(i + r, 4)
            total = None
            for a in range(3):
                part = hid[pl.ds(y + a, 8), m0:m1].reshape(8 * columns, 3 * HID)
                term = jnp.dot(part, mid_k[a], preferred_element_type=F32)
                total = term if total is None else total + term
            middle = jnp.maximum(total + mid_b[...], 0.0).astype(BF16)
            flow = lax.dot_general(flow_w[...], middle, NT, preferred_element_type=F32)
            for c in range(2):
                for n in range(8):
                    out[0, c, pl.ds(y + n, 1), m0:m1] = (
                        flow[c : c + 1, n * columns : (n + 1) * columns] + flow_b[c]
                    )
            return carry

        lax.fori_loop(0, 3, head, 0)
        rim.wait_send()
        rim_in.wait_recv()
        head(3, 0)

    for k in range(len(PARTS)):
        do_part(k)

    for k in range(len(PARTS)):
        for j in group_order:
            for kind in range(5):
                row_copy(kind, k, j).wait_send()


def on_device(
    tiles,
    frames,
    feat_weight,
    feat_bias,
    send_rows,
    recv_slots,
    blend,
    corr_weight,
    corr_bias,
    mid_weight,
    mid_bias,
    flow_weight,
    flow_bias,
):
    vmem = pl.BlockSpec(memory_space=pltpu.VMEM)
    smem = pl.BlockSpec(memory_space=pltpu.SMEM)
    hbm = pl.BlockSpec(memory_space=pl.ANY)
    dma = pltpu.SemaphoreType.DMA
    parts = len(PARTS)
    return pl.pallas_call(
        functools.partial(kernel, tiles),
        out_shape=jax.ShapeDtypeStruct((1, 2, BAND, WIDTH), F32),
        in_specs=[hbm, vmem, vmem, vmem, smem, smem, vmem, vmem, vmem, hbm, vmem, vmem, smem],
        out_specs=vmem,
        scratch_shapes=[
            pltpu.VMEM((2, 4, CIN, 16, 2 * WIDTH), BF16),
            pltpu.VMEM((2 * WIDTH, 3 * WIDTH), BF16),
            pltpu.VMEM((CH, 9 * CIN), BF16),
            pltpu.VMEM((3, 16 * CIN, WIDTH), F32),
            pltpu.VMEM((2, 66, 3 * CIN, WIDTH), BF16),
            pltpu.VMEM((CH, CH), F32),
            pltpu.VMEM((6, 2 * BAND, PARTS[0][0][1] - PARTS[0][0][0], CH), BF16),
            pltpu.VMEM((6, 2 * BAND, PARTS[1][0][1] - PARTS[1][0][0], CH), BF16),
            pltpu.VMEM((6, 3, 2, BAND), jnp.int32),
            pltpu.SMEM((6, 3, 2, BAND), jnp.int32),
            pltpu.VMEM((BAND, WIDTH, CH), BF16),
            pltpu.VMEM((BAND, WIDTH, CH), BF16),
            pltpu.VMEM((BAND + 16, CH, WIDTH), BF16),
            pltpu.VMEM((8, WIDTH, CH), BF16),
            pltpu.VMEM((WIDTH, WIDTH), BF16),
            pltpu.VMEM((BAND, WIDTH, 2 * WIDTH), F32),
            pltpu.VMEM((2 * WIDTH, HID), BF16),
            pltpu.VMEM((BAND, 16, HID), F32),
            pltpu.VMEM((BAND + 2, WIDTH, 3 * HID), BF16),
            pltpu.VMEM((9, MID, HID), BF16),
            pltpu.VMEM((3, 3 * HID, MID), BF16),
            dma((8,)),
            dma((2,)),
            dma((2,)),
            dma((5, parts, GROUPS)),
            dma((5, parts, GROUPS)),
            dma((5,)),
            dma((5,)),
            dma((2, parts)),
            dma((2, parts)),
            dma((2,)),
        ],
        compiler_params=pltpu.CompilerParams(
            collective_id=0, has_side_effects=True, vmem_limit_bytes=60 * 1024 * 1024
        ),
    )(
        frames,
        feat_weight.transpose(0, 2, 1).reshape(9 * CIN, CH),
        feat_bias.reshape(1, CH),
        send_rows,
        recv_slots.transpose(0, 1, 3, 2),
        blend.transpose(0, 1, 3, 2),
        jnp.asarray(offset_lanes(), BF16),
        corr_weight.T,
        corr_bias.reshape(1, HID),
        mid_weight,
        mid_bias.reshape(1, MID),
        flow_weight,
        flow_bias,
    )


def solution(mesh):
    return jax.shard_map(
        functools.partial(on_device, mesh.shape["tiles"]),
        mesh=mesh,
        in_specs=(
            P("tiles", None, None, "rows", None),
            P(),
            P(),
            P("tiles", "rows", None, None, None),
            P("tiles", "rows", None, None),
            P("tiles", "rows", None, None),
            P(),
            P(),
            P(),
            P(),
            P(),
            P(),
        ),
        out_specs=P("tiles", None, "rows", None),
        check_vma=False,
    )
```

```python
import functools

import jax
import jax.numpy as jnp
import numpy as np
from jax import lax
from jax.experimental import pallas as pl
from jax.experimental.pallas import tpu as pltpu
from jax.sharding import PartitionSpec as P

BF16 = jnp.bfloat16
F32 = jnp.float32
MESH = pl.DeviceIdType.MESH

CIN = 64
CH = 128
HID = 256
MID = 192
WIDTH = 128
BAND = 32
GROUP = 8
GROUPS = 2 * BAND // GROUP
SPAN = 9
NT = (((1,), (1,)), ((), ()))
TN = (((0,), (0,)), ((), ()))

PARTS = (
    ((0, 80), (0, 64), (0, 48)),
    ((80, 128), (64, 128), (48, 128)),

)


def centre_of(step_row):
    return 24 * (step_row % 5) + 15


def offset_lanes():
    lanes = np.zeros((2 * WIDTH, SPAN * SPAN), np.float32)
    for offset in range(SPAN * SPAN):
        step_row, step_col = offset // SPAN, offset % SPAN
        lanes[WIDTH * (step_row // 5) + centre_of(step_row) + 8 - 2 * step_col, offset] = 1.0
    return lanes


def kernel(
    tiles,
    frames,
    feat_w,
    feat_b,
    sent,
    slots,
    blend,
    lanes,
    corr_w,
    corr_b,
    mid_w,
    mid_b,
    flow_w,
    flow_b,
    out,
    xin,
    picks,
    conv_w,
    split,
    taps,
    bias_t,
    *rest,
):
    rows, rest = rest[: len(PARTS)], rest[len(PARTS) :]
    run(tiles, frames, feat_w, feat_b, sent, slots, blend, lanes, corr_w, corr_b, mid_w, mid_b,
        flow_w, flow_b, out, xin, picks, conv_w, split, taps, bias_t, rows, *rest)


def run(
    tiles,
    frames,
    feat_w,
    feat_b,
    sent,
    slots,
    blend,
    lanes,
    corr_w,
    corr_b,
    mid_w,
    mid_b,
    flow_w,
    flow_b,
    out,
    xin,
    picks,
    conv_w,
    split,
    taps,
    bias_t,
    rows,
    table_v,
    table_s,
    row_of,
    weight_of,
    g0,
    g1,
    g1_t,
    halo,
    mirror,
    packed,
    corr_k,
    tail,
    hid,
    mid_in,
    mid_k,
    in_sem,
    halo_send,
    halo_recv,
    row_send,
    row_recv,
    table_send,
    table_recv,
    edge_send,
    edge_recv,
    local_sem,
):
    t = lax.axis_index("tiles")
    r = lax.axis_index("rows")
    right, left = lax.rem(t + 1, tiles), lax.rem(t + tiles - 1, tiles)
    other = 1 - r

    order = [(f, g) for f in range(2) for g in (3, 2, 1, 0)]
    loads = {}
    for f, g in order:
        loads[f, g] = pltpu.make_async_copy(
            frames.at[0, f, :, pl.ds(16 * g, 16), :], xin.at[f, g], in_sem.at[4 * f + g]
        )
        loads[f, g].start()
    mid_load = pltpu.make_async_copy(mid_w, mid_in, local_sem.at[0])
    mid_load.start()

    peers = [(right, r), (left, r), (t, other), (right, other), (left, other)]
    barrier = pltpu.get_barrier_semaphore()
    for peer in peers:
        pl.semaphore_signal(barrier, inc=1, device_id=peer, device_id_type=MESH)

    column = lax.broadcasted_iota(jnp.int32, (2 * WIDTH, WIDTH), 0)
    target = lax.broadcasted_iota(jnp.int32, (2 * WIDTH, WIDTH), 1)
    for b in range(3):
        picks[:, b * WIDTH : (b + 1) * WIDTH] = jnp.where(column == 2 * target - 1 + b, 1.0, 0.0).astype(BF16)
    conv_w[...] = feat_w[...].T
    bias_t[...] = jnp.broadcast_to(feat_b[...], (CH, CH)).T
    taps[:, 0] = jnp.zeros((2, 3 * CIN, WIDTH), BF16)

    def split_group(f, g):
        loads[f, g].wait()

        def columns(i, carry):
            part = xin[f, g, pl.ds(16 * i, 16)].reshape(256, 2 * WIDTH)
            found = jnp.dot(part, picks[...], preferred_element_type=F32)
            for b in range(3):
                split[b, pl.ds(256 * i, 256), :] = found[:, b * WIDTH : (b + 1) * WIDTH]
            return carry

        lax.fori_loop(0, 4, columns, 0, unroll=2)

        def regroup(i, carry):
            for b in range(3):
                taps[f, 1 + 16 * g + i, b * CIN : (b + 1) * CIN, :] = split[
                    b, pl.ds(i, CIN, stride=16), :
                ].astype(BF16)
            return carry

        lax.fori_loop(0, 16, regroup, 0, unroll=8)

    def conv_group(f, g):
        def pair(p, carry):
            y = 8 * g + 2 * p
            upper = taps[f, pl.ds(2 * y, 3)].reshape(9 * CIN, WIDTH)
            lower = taps[f, pl.ds(2 * y + 2, 3)].reshape(9 * CIN, WIDTH)
            found = jnp.dot(
                conv_w[...],
                jnp.concatenate([upper, lower], axis=1),
                preferred_element_type=F32,
            )
            for i in range(2):
                feature = found[:, i * WIDTH : (i + 1) * WIDTH] + bias_t[...]
                feature = jnp.maximum(feature, 0.0).astype(BF16).T
                for k in range(len(PARTS)):
                    low, high = PARTS[k][0]
                    rows[k][2 * BAND * (2 + r) + f * BAND + y + i] = feature[low:high]
            return carry

        lax.fori_loop(0, 4, pair, 0, unroll=2)

    def remote(src, dst, send, recv, peer):
        return pltpu.make_async_remote_copy(
            src_ref=src, dst_ref=dst, send_sem=send, recv_sem=recv, device_id=peer, device_id_type=MESH
        )

    def row_copy(kind, k, j):
        window = 2 * (2, 0, 1, 2, 0)[kind] + r
        place = 2 * (1, 1, 1, 2, 0)[kind] + r
        peer = ((right, r), (left, r), (t, other), (t, other), (t, other))[kind]
        return remote(
            rows[k].at[pl.ds(2 * BAND * place + GROUP * j, GROUP)],
            rows[k].at[pl.ds(2 * BAND * window + GROUP * j, GROUP)],
            row_send.at[kind, k, j],
            row_recv.at[kind, k, j],
            peer,
        )

    table_v[2 + r] = sent[0, 0]
    halos = [
        remote(taps.at[f, 64], taps.at[f, 65], halo_send.at[f], halo_recv.at[f], (t, other))
        for f in range(2)
    ]
    tables = []
    for i, peer in enumerate(peers):
        window = (4, 0, 2, 4, 0)[i] + r
        tables.append(remote(table_v.at[2 + r], table_v.at[window], table_send.at[i], table_recv.at[i], peer))

    split_group(0, 3)
    pl.semaphore_wait(barrier, 5)
    for f in range(2):
        if f:
            split_group(f, 3)
        halos[f].start()
        for g in (3, 2, 1, 0):
            if g:
                split_group(f, g - 1)
            else:
                halos[f].wait()
                above = taps[f, 65]
                taps[f, 0] = jnp.where(r == 0, jnp.zeros_like(above), above)
            conv_group(f, g)
            for kind in range(3):
                row_copy(kind, 0, 4 * f + g).start()
        if f == 0:
            for copy in tables:
                copy.start()
    group_order = [4 * f + g for f, g in order]
    for k in range(1, len(PARTS)):
        for j in group_order:
            for kind in range(3):
                row_copy(kind, k, j).start()

    lane = lax.broadcasted_iota(jnp.int32, (WIDTH, WIDTH), 1)
    place = lax.broadcasted_iota(jnp.int32, (WIDTH, WIDTH), 0)
    mirror[...] = jnp.where(lane == WIDTH - 1 - place, 1.0, 0.0).astype(BF16)
    corr_k[...] = jnp.dot(lanes[...], corr_w[...], preferred_element_type=F32).astype(BF16)
    hid[33 * r] = jnp.zeros((WIDTH, 3 * HID), BF16)

    def clear(i, carry):
        packed[i] = jnp.zeros((WIDTH, 2 * WIDTH), F32)
        return carry

    lax.fori_loop(0, BAND, clear, 0)

    def clear_rim(i, carry):
        g1_t[i % 2 * 24 + 20 * r + i // 2] = jnp.zeros((CH, WIDTH), BF16)
        return carry

    lax.fori_loop(0, 8, clear_rim, 0)
    mid_load.wait()
    for tap in range(9):
        a, b = tap // 3, tap % 3
        mid_k[a, b * HID : (b + 1) * HID, :] = mid_in[tap].T

    for copy in tables:
        copy.wait()
    to_scalar = pltpu.make_async_copy(table_v, table_s, local_sem.at[1])
    to_scalar.start()
    to_scalar.wait()

    def look_up(j, carry):
        for i in range(2):
            slot = slots[0, 0, i, j]
            window = slot // BAND
            row = table_s[window, window // 2, r, slot % BAND]
            row_of[i, j] = 2 * BAND * window + jnp.minimum(row, 2 * BAND - 1)
            weight_of[i, j] = jnp.where(row < 2 * BAND, blend[0, 0, i, j], 0.0)
        return carry

    lax.fori_loop(0, 2 * BAND, look_up, 0, unroll=4)

    lane8 = lax.broadcasted_iota(jnp.int32, (8, WIDTH), 1)
    place8 = lax.broadcasted_iota(jnp.int32, (8, WIDTH), 0)

    def forward(k):
        for j in group_order:
            for kind in range(2):
                row_copy(kind, k, j).wait_recv()
                row_copy(3 + kind, k, j).start()

    def do_part(k):
        (a0, a1), (c0, c1), (m0, m1) = PARTS[k]
        width = c1 - c0

        forward(k)
        for j in group_order:
            for kind in (2, 3, 4):
                row_copy(kind, k, j).wait_recv()

        def source(j, i):
            return weight_of[i, j] * rows[k][row_of[i, j]].astype(F32)

        def turn(where, value):
            turned = lax.dot_general(value, mirror[a0:a1], TN, preferred_element_type=F32).astype(BF16)
            if k:
                turned = g1_t[where] + turned
            g1_t[where] = turned

        def ground(i, carry):
            y = lax.rem(24 * other + i, BAND)
            parity, half = lax.rem(y, 2), y // 2
            g0[16 * parity + half, a0:a1] = (source(y, 0) + source(y, 1)).astype(BF16)
            second = (source(BAND + y, 0) + source(BAND + y, 1)).astype(BF16)
            g1[y, a0:a1] = second
            turn(24 * parity + 4 + half, second)
            return carry

        lax.fori_loop(0, 8, ground, 0, unroll=4)
        edge = remote(
            g1.at[pl.ds(24 * other, 8), pl.ds(a0, a1 - a0)],
            halo.at[:, pl.ds(a0, a1 - a0)],
            edge_send.at[0, k],
            edge_recv.at[0, k],
            (t, other),
        )
        edge.start()
        lax.fori_loop(8, BAND, ground, 0, unroll=4)
        edge.wait()

        def ground_halo(i, carry):
            turn(24 * lax.rem(i, 2) + 20 * other + i // 2, halo[i, a0:a1])
            return carry

        lax.fori_loop(0, 8, ground_halo, 0, unroll=8)

        def correlate(b, carry):
            parity, block = lax.rem(b, 2), b // 2
            first = 16 * parity + 4 * block
            second = 24 * parity + 4 * block
            for j in range(0, 12, 2):
                low, high = max(0, j - 8), min(4, j + 2)
                left_side = g0[pl.ds(first + low, high - low), c0:c1].reshape((high - low) * width, CH)
                pair = jnp.concatenate([g1_t[second + j], g1_t[second + j + 1]], axis=1)
                found = jnp.dot(left_side, pair, preferred_element_type=F32)
                for h in range(low, high):
                    for e in range(2):
                        u = j + e - h
                        if not 0 <= u < SPAN:
                            continue
                        centre = centre_of(u)
                        for x in range(c0, c1, 8):
                            at = (h - low) * width + x - c0
                            turned = pltpu.roll(
                                found[at : at + 8, e * WIDTH : (e + 1) * WIDTH],
                                (centre + 1 + x) % WIDTH,
                                1,
                                stride=1,
                                stride_axis=0,
                            )
                            mask = (lane8 >= centre - 8) & (lane8 <= centre + 8)
                            if x == 0:
                                mask = mask & (place8 + centre - lane8 >= 0)
                            if x == WIDTH - 8:
                                mask = mask & (place8 + centre - lane8 < 8)
                            pltpu.store(
                                packed.at[
                                    first + h, pl.ds(x, 8), pl.ds(WIDTH * (u // 5), WIDTH)
                                ],
                                turned,
                                mask=mask,
                            )
            return carry

        lax.fori_loop(0, 8, correlate, 0, unroll=2)

        kept = 16 if k else 0
        side = lax.broadcasted_iota(jnp.int32, (width + kept, HID), 0)

        def hidden(q, carry):
            scaled = (packed[pl.ds(4 * q, 4), c0:c1] * CH**-0.5).astype(BF16).reshape(4 * width, 2 * WIDTH)
            found = jnp.dot(scaled, corr_k[...], preferred_element_type=F32)
            found = jnp.maximum(found + corr_b[...], 0.0)
            for n in range(4):
                i = 4 * q + n
                at = 2 * lax.rem(i, 16) + i // 16 + 1
                value = found[n * width : (n + 1) * width]
                whole = jnp.concatenate([tail[i], value], axis=0) if k else value
                before = pltpu.roll(whole, 1, 0)
                after = pltpu.roll(whole, width + kept - 1, 0)
                if k == 0:
                    before = jnp.where(side == 0, 0.0, before)
                if k == len(PARTS) - 1:
                    after = jnp.where(side == width + kept - 1, 0.0, after)
                else:
                    tail[i] = value[width - 16 :]
                hid[at, c0:c1, 0:HID] = before[kept:].astype(BF16)
                hid[at, c0:c1, HID : 2 * HID] = value.astype(BF16)
                hid[at, m0:m1, 2 * HID : 3 * HID] = after[0 : m1 - m0].astype(BF16)
            return carry

        lax.fori_loop(0, BAND // 4, hidden, 0, unroll=2)

        rim = remote(
            hid.at[32 - 31 * r, pl.ds(m0, m1 - m0)],
            hid.at[33 * r, pl.ds(m0, m1 - m0)],
            edge_send.at[1, k],
            edge_recv.at[1, k],
            (t, other),
        )
        rim_in = remote(
            hid.at[32 - 31 * r, pl.ds(m0, m1 - m0)],
            hid.at[33 * other, pl.ds(m0, m1 - m0)],
            edge_send.at[1, k],
            edge_recv.at[1, k],
            (t, other),
        )
        rim.start()
        columns = m1 - m0

        def head(i, carry):
            y = 8 * lax.rem(i + r, 4)
            total = None
            for a in range(3):
                part = hid[pl.ds(y + a, 8), m0:m1].reshape(8 * columns, 3 * HID)
                term = jnp.dot(part, mid_k[a], preferred_element_type=F32)
                total = term if total is None else total + term
            middle = jnp.maximum(total + mid_b[...], 0.0).astype(BF16)
            flow = lax.dot_general(flow_w[...], middle, NT, preferred_element_type=F32)
            for c in range(2):
                for n in range(8):
                    out[0, c, pl.ds(y + n, 1), m0:m1] = (
                        flow[c : c + 1, n * columns : (n + 1) * columns] + flow_b[c]
                    )
            return carry

        lax.fori_loop(0, 3, head, 0)
        rim.wait_send()
        rim_in.wait_recv()
        head(3, 0)

    for k in range(len(PARTS)):
        do_part(k)

    for k in range(len(PARTS)):
        for j in group_order:
            for kind in range(5):
                row_copy(kind, k, j).wait_send()


def on_device(
    tiles,
    frames,
    feat_weight,
    feat_bias,
    send_rows,
    recv_slots,
    blend,
    corr_weight,
    corr_bias,
    mid_weight,
    mid_bias,
    flow_weight,
    flow_bias,
):
    vmem = pl.BlockSpec(memory_space=pltpu.VMEM)
    smem = pl.BlockSpec(memory_space=pltpu.SMEM)
    hbm = pl.BlockSpec(memory_space=pl.ANY)
    dma = pltpu.SemaphoreType.DMA
    parts = len(PARTS)
    return pl.pallas_call(
        functools.partial(kernel, tiles),
        out_shape=jax.ShapeDtypeStruct((1, 2, BAND, WIDTH), F32),
        in_specs=[hbm, vmem, vmem, vmem, smem, smem, vmem, vmem, vmem, hbm, vmem, vmem, smem],
        out_specs=vmem,
        scratch_shapes=[
            pltpu.VMEM((2, 4, CIN, 16, 2 * WIDTH), BF16),
            pltpu.VMEM((2 * WIDTH, 3 * WIDTH), BF16),
            pltpu.VMEM((CH, 9 * CIN), BF16),
            pltpu.VMEM((3, 16 * CIN, WIDTH), F32),
            pltpu.VMEM((2, 66, 3 * CIN, WIDTH), BF16),
            pltpu.VMEM((CH, CH), F32),
            *[pltpu.VMEM((12 * BAND, high - low, CH), BF16) for (low, high), _, _ in PARTS],
            pltpu.VMEM((6, 3, 2, BAND), jnp.int32),
            pltpu.SMEM((6, 3, 2, BAND), jnp.int32),
            pltpu.SMEM((2, 2 * BAND), jnp.int32),
            pltpu.SMEM((2, 2 * BAND), F32),
            pltpu.VMEM((BAND, WIDTH, CH), BF16),
            pltpu.VMEM((BAND, WIDTH, CH), BF16),
            pltpu.VMEM((BAND + 16, CH, WIDTH), BF16),
            pltpu.VMEM((8, WIDTH, CH), BF16),
            pltpu.VMEM((WIDTH, WIDTH), BF16),
            pltpu.VMEM((BAND, WIDTH, 2 * WIDTH), F32),
            pltpu.VMEM((2 * WIDTH, HID), BF16),
            pltpu.VMEM((BAND, 16, HID), F32),
            pltpu.VMEM((BAND + 2, WIDTH, 3 * HID), BF16),
            pltpu.VMEM((9, MID, HID), BF16),
            pltpu.VMEM((3, 3 * HID, MID), BF16),
            dma((8,)),
            dma((2,)),
            dma((2,)),
            dma((5, parts, GROUPS)),
            dma((5, parts, GROUPS)),
            dma((5,)),
            dma((5,)),
            dma((2, parts)),
            dma((2, parts)),
            dma((2,)),
        ],
        compiler_params=pltpu.CompilerParams(
            collective_id=0, has_side_effects=True, vmem_limit_bytes=60 * 1024 * 1024
        ),
    )(
        frames,
        feat_weight.transpose(0, 2, 1).reshape(9 * CIN, CH),
        feat_bias.reshape(1, CH),
        send_rows,
        recv_slots.transpose(0, 1, 3, 2),
        blend.transpose(0, 1, 3, 2),
        jnp.asarray(offset_lanes(), BF16),
        corr_weight.T,
        corr_bias.reshape(1, HID),
        mid_weight,
        mid_bias.reshape(1, MID),
        flow_weight,
        flow_bias,
    )


def solution(mesh):
    return jax.shard_map(
        functools.partial(on_device, mesh.shape["tiles"]),
        mesh=mesh,
        in_specs=(
            P("tiles", None, None, "rows", None),
            P(),
            P(),
            P("tiles", "rows", None, None, None),
            P("tiles", "rows", None, None),
            P("tiles", "rows", None, None),
            P(),
            P(),
            P(),
            P(),
            P(),
            P(),
        ),
        out_specs=P("tiles", None, "rows", None),
        check_vma=False,
    )
```

```python
import functools

import jax
import jax.numpy as jnp
import numpy as np
from jax import lax
from jax.experimental import pallas as pl
from jax.experimental.pallas import tpu as pltpu
from jax.sharding import PartitionSpec as P

BF16 = jnp.bfloat16
F32 = jnp.float32
MESH = pl.DeviceIdType.MESH

CIN = 64
CH = 128
HID = 256
MID = 192
WIDTH = 128
BAND = 32
SPAN = 9
NT = (((1,), (1,)), ((), ()))
TN = (((0,), (0,)), ((), ()))

PARTS = (
    ((0, 80), (0, 64), (0, 48)),
    ((80, 128), (64, 128), (48, 128)),

)


UNITS = tuple(
    (f * BAND + first, count)
    for f in range(2)
    for first, count in ((29, 3), (25, 4), (17, 8), (9, 8), (1, 8), (0, 1))
)
GROUPS = len(UNITS)


def centre_of(step_row):
    return 24 * (step_row % 5) + 15


def offset_lanes():
    lanes = np.zeros((2 * WIDTH, SPAN * SPAN), np.float32)
    for offset in range(SPAN * SPAN):
        step_row, step_col = offset // SPAN, offset % SPAN
        lanes[WIDTH * (step_row // 5) + centre_of(step_row) + 8 - 2 * step_col, offset] = 1.0
    return lanes


def kernel(
    tiles,
    frames,
    feat_w,
    feat_b,
    sent,
    slots,
    blend,
    lanes,
    corr_w,
    corr_b,
    mid_w,
    mid_b,
    flow_w,
    flow_b,
    out,
    xin,
    picks,
    conv_w,
    split,
    taps,
    bias_t,
    *buffers,
):
    rows, buffers = buffers[: len(PARTS)], buffers[len(PARTS) :]
    (
        table_v,
        table_s,
        row_of,
        weight_of,
        g0,
        g1,
        g1_t,
        halo,
        mirror,
        packed,
        corr_k,
        tail,
        hid,
        mid_in,
        mid_k,
        in_sem,
        halo_send,
        halo_recv,
        row_send,
        row_recv,
        table_send,
        table_recv,
        edge_send,
        edge_recv,
        local_sem,
    ) = buffers
    t = lax.axis_index("tiles")
    r = lax.axis_index("rows")
    right, left = lax.rem(t + 1, tiles), lax.rem(t + tiles - 1, tiles)
    other = 1 - r

    order = [(f, g) for f in range(2) for g in (3, 2, 1, 0)]
    loads = {}
    for f, g in order:
        loads[f, g] = pltpu.make_async_copy(
            frames.at[0, f, :, pl.ds(16 * g, 16), :], xin.at[f, g], in_sem.at[4 * f + g]
        )
        loads[f, g].start()
    mid_load = pltpu.make_async_copy(mid_w, mid_in, local_sem.at[0])
    mid_load.start()

    peers = [(right, r), (left, r), (t, other), (right, other), (left, other)]
    barrier = pltpu.get_barrier_semaphore()
    for peer in peers:
        pl.semaphore_signal(barrier, inc=1, device_id=peer, device_id_type=MESH)

    column = lax.broadcasted_iota(jnp.int32, (2 * WIDTH, WIDTH), 0)
    target = lax.broadcasted_iota(jnp.int32, (2 * WIDTH, WIDTH), 1)
    for b in range(3):
        picks[:, b * WIDTH : (b + 1) * WIDTH] = jnp.where(column == 2 * target - 1 + b, 1.0, 0.0).astype(BF16)
    conv_w[...] = feat_w[...].T
    bias_t[...] = jnp.broadcast_to(feat_b[...], (CH, CH)).T
    taps[:, 0] = jnp.zeros((2, 3 * CIN, WIDTH), BF16)

    def split_group(f, g):
        loads[f, g].wait()

        def columns(i, carry):
            part = xin[f, g, pl.ds(16 * i, 16)].reshape(256, 2 * WIDTH)
            found = jnp.dot(part, picks[...], preferred_element_type=F32)
            for b in range(3):
                split[b, pl.ds(256 * i, 256), :] = found[:, b * WIDTH : (b + 1) * WIDTH]
            return carry

        lax.fori_loop(0, 4, columns, 0, unroll=2)

        def regroup(i, carry):
            for b in range(3):
                taps[f, 1 + 16 * g + i, b * CIN : (b + 1) * CIN, :] = split[
                    b, pl.ds(i, CIN, stride=16), :
                ].astype(BF16)
            return carry

        lax.fori_loop(0, 16, regroup, 0, unroll=8)

    def conv_rows(f, y, count):
        tiles_in = [taps[f, pl.ds(2 * (y + n), 3)].reshape(9 * CIN, WIDTH) for n in range(count)]
        found = jnp.dot(conv_w[...], jnp.concatenate(tiles_in, axis=1), preferred_element_type=F32)
        for n in range(count):
            feature = found[:, n * WIDTH : (n + 1) * WIDTH] + bias_t[...]
            feature = jnp.maximum(feature, 0.0).astype(BF16).T
            for k in range(len(PARTS)):
                low, high = PARTS[k][0]
                rows[k][2 * BAND * (2 + r) + f * BAND + y + n] = feature[low:high]

    def conv_pairs(f, y, pairs):
        def pair(p, carry):
            conv_rows(f, y + 2 * p, 2)
            return carry

        lax.fori_loop(0, pairs, pair, 0, unroll=2)

    def remote(src, dst, send, recv, peer):
        return pltpu.make_async_remote_copy(
            src_ref=src, dst_ref=dst, send_sem=send, recv_sem=recv, device_id=peer, device_id_type=MESH
        )

    def row_copy(kind, k, j):
        window = 2 * (2, 0, 1, 2, 0)[kind] + r
        place = 2 * (1, 1, 1, 2, 0)[kind] + r
        peer = ((right, r), (left, r), (t, other), (t, other), (t, other))[kind]
        first, count = UNITS[j]
        return remote(
            rows[k].at[pl.ds(2 * BAND * place + first, count)],
            rows[k].at[pl.ds(2 * BAND * window + first, count)],
            row_send.at[kind, k, j],
            row_recv.at[kind, k, j],
            peer,
        )

    table_v[2 + r] = sent[0, 0]
    halos = [
        remote(taps.at[f, 64], taps.at[f, 65], halo_send.at[f], halo_recv.at[f], (t, other))
        for f in range(2)
    ]
    tables = []
    for i, peer in enumerate(peers):
        window = (4, 0, 2, 4, 0)[i] + r
        tables.append(remote(table_v.at[2 + r], table_v.at[window], table_send.at[i], table_recv.at[i], peer))

    def send(k, j):
        for kind in range(3):
            row_copy(kind, k, j).start()

    for f in range(2):
        base = 6 * f
        split_group(f, 3)
        conv_rows(f, 31, 1)
        conv_rows(f, 29, 2)
        if f == 0:
            pl.semaphore_wait(barrier, 5)
        send(0, base)
        halos[f].start()
        conv_pairs(f, 25, 2)
        send(0, base + 1)
        for n, g in enumerate((2, 1, 0)):
            split_group(f, g)
            conv_pairs(f, 8 * g + 1, 4)
            send(0, base + 2 + n)
        halos[f].wait()
        above = taps[f, 65]
        taps[f, 0] = jnp.where(r == 0, jnp.zeros_like(above), above)
        conv_rows(f, 0, 1)
        send(0, base + 5)
        if f == 0:
            for copy in tables:
                copy.start()
    group_order = range(GROUPS)
    for k in range(1, len(PARTS)):
        for j in group_order:
            for kind in range(3):
                row_copy(kind, k, j).start()

    lane = lax.broadcasted_iota(jnp.int32, (WIDTH, WIDTH), 1)
    place = lax.broadcasted_iota(jnp.int32, (WIDTH, WIDTH), 0)
    mirror[...] = jnp.where(lane == WIDTH - 1 - place, 1.0, 0.0).astype(BF16)
    corr_k[...] = jnp.dot(lanes[...], corr_w[...], preferred_element_type=F32).astype(BF16)
    hid[33 * r] = jnp.zeros((WIDTH, 3 * HID), BF16)

    def clear(i, carry):
        packed[i] = jnp.zeros((WIDTH, 2 * WIDTH), F32)
        return carry

    lax.fori_loop(0, BAND, clear, 0)

    def clear_rim(i, carry):
        g1_t[i % 2 * 24 + 20 * r + i // 2] = jnp.zeros((CH, WIDTH), BF16)
        return carry

    lax.fori_loop(0, 8, clear_rim, 0)
    mid_load.wait()
    for tap in range(9):
        mid_k[tap * HID : (tap + 1) * HID, :] = mid_in[tap].T

    for copy in tables:
        copy.wait()
    to_scalar = pltpu.make_async_copy(table_v, table_s, local_sem.at[1])
    to_scalar.start()
    to_scalar.wait()

    def look_up(j, carry):
        for i in range(2):
            slot = slots[0, 0, i, j]
            window = slot // BAND
            row = table_s[window, window // 2, r, slot % BAND]
            row_of[i, j] = 2 * BAND * window + jnp.minimum(row, 2 * BAND - 1)
            weight_of[i, j] = jnp.where(row < 2 * BAND, blend[0, 0, i, j], 0.0)
        return carry

    lax.fori_loop(0, 2 * BAND, look_up, 0, unroll=4)

    lane8 = lax.broadcasted_iota(jnp.int32, (8, WIDTH), 1)
    place8 = lax.broadcasted_iota(jnp.int32, (8, WIDTH), 0)

    def forward(k):
        for j in group_order:
            for kind in range(2):
                row_copy(kind, k, j).wait_recv()
                row_copy(3 + kind, k, j).start()

    def do_part(k):
        (a0, a1), (c0, c1), (m0, m1) = PARTS[k]
        width = c1 - c0

        forward(k)
        for j in group_order:
            for kind in (2, 3, 4):
                row_copy(kind, k, j).wait_recv()

        def source(j, i):
            return weight_of[i, j] * rows[k][row_of[i, j]].astype(F32)

        def turn(where, value):
            turned = lax.dot_general(value, mirror[a0:a1], TN, preferred_element_type=F32).astype(BF16)
            if k:
                turned = g1_t[where] + turned
            g1_t[where] = turned

        def ground(i, carry):
            y = lax.rem(24 * other + i, BAND)
            parity, half = lax.rem(y, 2), y // 2
            g0[16 * parity + half, a0:a1] = (source(y, 0) + source(y, 1)).astype(BF16)
            second = (source(BAND + y, 0) + source(BAND + y, 1)).astype(BF16)
            g1[y, a0:a1] = second
            turn(24 * parity + 4 + half, second)
            return carry

        lax.fori_loop(0, 8, ground, 0, unroll=4)
        edge = remote(
            g1.at[pl.ds(24 * other, 8), pl.ds(a0, a1 - a0)],
            halo.at[:, pl.ds(a0, a1 - a0)],
            edge_send.at[0, k],
            edge_recv.at[0, k],
            (t, other),
        )
        edge.start()
        lax.fori_loop(8, BAND, ground, 0, unroll=4)
        edge.wait()

        def ground_halo(i, carry):
            turn(24 * lax.rem(i, 2) + 20 * other + i // 2, halo[i, a0:a1])
            return carry

        lax.fori_loop(0, 8, ground_halo, 0, unroll=8)

        def correlate(b, carry):
            parity, block = lax.rem(b, 2), b // 2
            first = 16 * parity + 4 * block
            second = 24 * parity + 4 * block
            for j in range(0, 12, 2):
                low, high = max(0, j - 8), min(4, j + 2)
                left_side = g0[pl.ds(first + low, high - low), c0:c1].reshape((high - low) * width, CH)
                pair = jnp.concatenate([g1_t[second + j], g1_t[second + j + 1]], axis=1)
                found = jnp.dot(left_side, pair, preferred_element_type=F32)
                for h in range(low, high):
                    for e in range(2):
                        u = j + e - h
                        if not 0 <= u < SPAN:
                            continue
                        centre = centre_of(u)
                        for x in range(c0, c1, 8):
                            at = (h - low) * width + x - c0
                            turned = pltpu.roll(
                                found[at : at + 8, e * WIDTH : (e + 1) * WIDTH],
                                (centre + 1 + x) % WIDTH,
                                1,
                                stride=1,
                                stride_axis=0,
                            )
                            mask = (lane8 >= centre - 8) & (lane8 <= centre + 8)
                            if x == 0:
                                mask = mask & (place8 + centre - lane8 >= 0)
                            if x == WIDTH - 8:
                                mask = mask & (place8 + centre - lane8 < 8)
                            pltpu.store(
                                packed.at[
                                    first + h, pl.ds(x, 8), pl.ds(WIDTH * (u // 5), WIDTH)
                                ],
                                turned,
                                mask=mask,
                            )
            return carry

        lax.fori_loop(0, 8, correlate, 0, unroll=2)

        kept = 16 if k else 0
        side = lax.broadcasted_iota(jnp.int32, (width + kept, HID), 0)

        def hidden(q, carry):
            scaled = (packed[pl.ds(4 * q, 4), c0:c1] * CH**-0.5).astype(BF16).reshape(4 * width, 2 * WIDTH)
            found = jnp.dot(scaled, corr_k[...], preferred_element_type=F32)
            found = jnp.maximum(found + corr_b[...], 0.0)
            for n in range(4):
                i = 4 * q + n
                at = 2 * lax.rem(i, 16) + i // 16 + 1
                value = found[n * width : (n + 1) * width]
                whole = jnp.concatenate([tail[i], value], axis=0) if k else value
                before = pltpu.roll(whole, 1, 0)
                after = pltpu.roll(whole, width + kept - 1, 0)
                if k == 0:
                    before = jnp.where(side == 0, 0.0, before)
                if k == len(PARTS) - 1:
                    after = jnp.where(side == width + kept - 1, 0.0, after)
                else:
                    tail[i] = value[width - 16 :]
                hid[at, c0:c1, 0:HID] = before[kept:].astype(BF16)
                hid[at, c0:c1, HID : 2 * HID] = value.astype(BF16)
                hid[at, m0:m1, 2 * HID : 3 * HID] = after[0 : m1 - m0].astype(BF16)
            return carry

        lax.fori_loop(0, BAND // 4, hidden, 0, unroll=2)

        rim = remote(
            hid.at[32 - 31 * r, pl.ds(m0, m1 - m0)],
            hid.at[33 * r, pl.ds(m0, m1 - m0)],
            edge_send.at[1, k],
            edge_recv.at[1, k],
            (t, other),
        )
        rim_in = remote(
            hid.at[32 - 31 * r, pl.ds(m0, m1 - m0)],
            hid.at[33 * other, pl.ds(m0, m1 - m0)],
            edge_send.at[1, k],
            edge_recv.at[1, k],
            (t, other),
        )
        rim.start()
        columns = m1 - m0

        def head(i, carry):
            y = 8 * lax.rem(i + r, 4)
            part = jnp.concatenate(
                [hid[pl.ds(y + a, 8), m0:m1].reshape(8 * columns, 3 * HID) for a in range(3)], axis=1
            )
            total = jnp.dot(part, mid_k[...], preferred_element_type=F32)
            middle = jnp.maximum(total + mid_b[...], 0.0).astype(BF16)
            flow = lax.dot_general(flow_w[...], middle, NT, preferred_element_type=F32)
            for c in range(2):
                for n in range(8):
                    out[0, c, pl.ds(y + n, 1), m0:m1] = (
                        flow[c : c + 1, n * columns : (n + 1) * columns] + flow_b[c]
                    )
            return carry

        lax.fori_loop(0, 3, head, 0)
        rim.wait_send()
        rim_in.wait_recv()
        head(3, 0)

    for k in range(len(PARTS)):
        do_part(k)

    for k in range(len(PARTS)):
        for j in group_order:
            for kind in range(5):
                row_copy(kind, k, j).wait_send()


def on_device(
    tiles,
    frames,
    feat_weight,
    feat_bias,
    send_rows,
    recv_slots,
    blend,
    corr_weight,
    corr_bias,
    mid_weight,
    mid_bias,
    flow_weight,
    flow_bias,
):
    vmem = pl.BlockSpec(memory_space=pltpu.VMEM)
    smem = pl.BlockSpec(memory_space=pltpu.SMEM)
    hbm = pl.BlockSpec(memory_space=pl.ANY)
    dma = pltpu.SemaphoreType.DMA
    parts = len(PARTS)
    return pl.pallas_call(
        functools.partial(kernel, tiles),
        out_shape=jax.ShapeDtypeStruct((1, 2, BAND, WIDTH), F32),
        in_specs=[hbm, vmem, vmem, vmem, smem, smem, vmem, vmem, vmem, hbm, vmem, vmem, smem],
        out_specs=vmem,
        scratch_shapes=[
            pltpu.VMEM((2, 4, CIN, 16, 2 * WIDTH), BF16),
            pltpu.VMEM((2 * WIDTH, 3 * WIDTH), BF16),
            pltpu.VMEM((CH, 9 * CIN), BF16),
            pltpu.VMEM((3, 16 * CIN, WIDTH), F32),
            pltpu.VMEM((2, 66, 3 * CIN, WIDTH), BF16),
            pltpu.VMEM((CH, CH), F32),
            *[pltpu.VMEM((12 * BAND, high - low, CH), BF16) for (low, high), _, _ in PARTS],
            pltpu.VMEM((6, 3, 2, BAND), jnp.int32),
            pltpu.SMEM((6, 3, 2, BAND), jnp.int32),
            pltpu.SMEM((2, 2 * BAND), jnp.int32),
            pltpu.SMEM((2, 2 * BAND), F32),
            pltpu.VMEM((BAND, WIDTH, CH), BF16),
            pltpu.VMEM((BAND, WIDTH, CH), BF16),
            pltpu.VMEM((BAND + 16, CH, WIDTH), BF16),
            pltpu.VMEM((8, WIDTH, CH), BF16),
            pltpu.VMEM((WIDTH, WIDTH), BF16),
            pltpu.VMEM((BAND, WIDTH, 2 * WIDTH), F32),
            pltpu.VMEM((2 * WIDTH, HID), BF16),
            pltpu.VMEM((BAND, 16, HID), F32),
            pltpu.VMEM((BAND + 2, WIDTH, 3 * HID), BF16),
            pltpu.VMEM((9, MID, HID), BF16),
            pltpu.VMEM((9 * HID, MID), BF16),
            dma((8,)),
            dma((2,)),
            dma((2,)),
            dma((5, parts, GROUPS)),
            dma((5, parts, GROUPS)),
            dma((5,)),
            dma((5,)),
            dma((2, parts)),
            dma((2, parts)),
            dma((2,)),
        ],
        compiler_params=pltpu.CompilerParams(
            collective_id=0, has_side_effects=True, vmem_limit_bytes=60 * 1024 * 1024
        ),
    )(
        frames,
        feat_weight.transpose(0, 2, 1).reshape(9 * CIN, CH),
        feat_bias.reshape(1, CH),
        send_rows,
        recv_slots.transpose(0, 1, 3, 2),
        blend.transpose(0, 1, 3, 2),
        jnp.asarray(offset_lanes(), BF16),
        corr_weight.T,
        corr_bias.reshape(1, HID),
        mid_weight,
        mid_bias.reshape(1, MID),
        flow_weight,
        flow_bias,
    )


def solution(mesh):
    return jax.shard_map(
        functools.partial(on_device, mesh.shape["tiles"]),
        mesh=mesh,
        in_specs=(
            P("tiles", None, None, "rows", None),
            P(),
            P(),
            P("tiles", "rows", None, None, None),
            P("tiles", "rows", None, None),
            P("tiles", "rows", None, None),
            P(),
            P(),
            P(),
            P(),
            P(),
            P(),
        ),
        out_specs=P("tiles", None, "rows", None),
        check_vma=False,
    )
```

```python
import functools

import jax
import jax.numpy as jnp
import numpy as np
from jax import lax
from jax.experimental import pallas as pl
from jax.experimental.pallas import tpu as pltpu
from jax.sharding import PartitionSpec as P

BF16 = jnp.bfloat16
F32 = jnp.float32
MESH = pl.DeviceIdType.MESH

CIN = 64
CH = 128
HID = 256
MID = 192
WIDTH = 128
BAND = 32
SPAN = 9
NT = (((1,), (1,)), ((), ()))
TN = (((0,), (0,)), ((), ()))

PARTS = (
    ((0, 80), (0, 64), (0, 48)),
    ((80, 128), (64, 128), (48, 128)),

)


UNITS = (
    tuple(
        (f * BAND + first, count)
        for f in range(2)
        for first, count in ((29, 3), (25, 4), (17, 8), (9, 8), (1, 8), (0, 1))
    ),
    ((0, 16), (16, 16), (32, 16), (48, 8), (56, 8)),
)
MOST = max(len(units) for units in UNITS)


def centre_of(step_row):
    return 24 * (step_row % 5) + 15


def offset_lanes():
    lanes = np.zeros((2 * WIDTH, SPAN * SPAN), np.float32)
    for offset in range(SPAN * SPAN):
        step_row, step_col = offset // SPAN, offset % SPAN
        lanes[WIDTH * (step_row // 5) + centre_of(step_row) + 8 - 2 * step_col, offset] = 1.0
    return lanes


def kernel(
    tiles,
    frames,
    feat_w,
    feat_b,
    sent,
    slots,
    blend,
    lanes,
    corr_w,
    corr_b,
    mid_w,
    mid_b,
    flow_w,
    flow_b,
    out,
    xin,
    picks,
    conv_w,
    split,
    taps,
    bias_t,
    *buffers,
):
    rows, buffers = buffers[: len(PARTS)], buffers[len(PARTS) :]
    (
        table_v,
        table_s,
        row_of,
        weight_of,
        g0,
        g1,
        g1_t,
        halo,
        mirror,
        packed,
        corr_k,
        tail,
        hid,
        mid_in,
        mid_k,
        in_sem,
        halo_send,
        halo_recv,
        row_send,
        row_recv,
        table_send,
        table_recv,
        edge_send,
        edge_recv,
        local_sem,
    ) = buffers
    t = lax.axis_index("tiles")
    r = lax.axis_index("rows")
    right, left = lax.rem(t + 1, tiles), lax.rem(t + tiles - 1, tiles)
    other = 1 - r

    order = [(f, g) for f in range(2) for g in (3, 2, 1, 0)]
    loads = {}
    for f, g in order:
        loads[f, g] = pltpu.make_async_copy(
            frames.at[0, f, :, pl.ds(16 * g, 16), :], xin.at[f, g], in_sem.at[4 * f + g]
        )
        loads[f, g].start()
    mid_load = pltpu.make_async_copy(mid_w, mid_in, local_sem.at[0])
    mid_load.start()

    peers = [(right, r), (left, r), (t, other), (right, other), (left, other)]
    barrier = pltpu.get_barrier_semaphore()
    for peer in peers:
        pl.semaphore_signal(barrier, inc=1, device_id=peer, device_id_type=MESH)

    column = lax.broadcasted_iota(jnp.int32, (2 * WIDTH, WIDTH), 0)
    target = lax.broadcasted_iota(jnp.int32, (2 * WIDTH, WIDTH), 1)
    for b in range(3):
        picks[:, b * WIDTH : (b + 1) * WIDTH] = jnp.where(column == 2 * target - 1 + b, 1.0, 0.0).astype(BF16)
    conv_w[...] = feat_w[...].T
    bias_t[...] = jnp.broadcast_to(feat_b[...], (CH, CH)).T
    taps[:, 0] = jnp.zeros((2, 3 * CIN, WIDTH), BF16)

    def split_group(f, g):
        loads[f, g].wait()

        def columns(i, carry):
            part = xin[f, g, pl.ds(16 * i, 16)].reshape(256, 2 * WIDTH)
            found = jnp.dot(part, picks[...], preferred_element_type=F32)
            for b in range(3):
                split[b, pl.ds(256 * i, 256), :] = found[:, b * WIDTH : (b + 1) * WIDTH]
            return carry

        lax.fori_loop(0, 4, columns, 0, unroll=2)

        def regroup(i, carry):
            for b in range(3):
                taps[f, 1 + 16 * g + i, b * CIN : (b + 1) * CIN, :] = split[
                    b, pl.ds(i, CIN, stride=16), :
                ].astype(BF16)
            return carry

        lax.fori_loop(0, 16, regroup, 0, unroll=8)

    def conv_rows(f, y, count):
        tiles_in = [taps[f, pl.ds(2 * (y + n), 3)].reshape(9 * CIN, WIDTH) for n in range(count)]
        found = jnp.dot(conv_w[...], jnp.concatenate(tiles_in, axis=1), preferred_element_type=F32)
        for n in range(count):
            feature = found[:, n * WIDTH : (n + 1) * WIDTH] + bias_t[...]
            feature = jnp.maximum(feature, 0.0).astype(BF16).T
            for k in range(len(PARTS)):
                low, high = PARTS[k][0]
                rows[k][2 * BAND * (2 + r) + f * BAND + y + n] = feature[low:high]

    def conv_pairs(f, y, pairs):
        def pair(p, carry):
            conv_rows(f, y + 2 * p, 2)
            return carry

        lax.fori_loop(0, pairs, pair, 0, unroll=2)

    def remote(src, dst, send, recv, peer):
        return pltpu.make_async_remote_copy(
            src_ref=src, dst_ref=dst, send_sem=send, recv_sem=recv, device_id=peer, device_id_type=MESH
        )

    def row_copy(kind, k, j):
        window = 2 * (2, 0, 1, 2, 0)[kind] + r
        place = 2 * (1, 1, 1, 2, 0)[kind] + r
        peer = ((right, r), (left, r), (t, other), (t, other), (t, other))[kind]
        first, count = UNITS[k][j]
        return remote(
            rows[k].at[pl.ds(2 * BAND * place + first, count)],
            rows[k].at[pl.ds(2 * BAND * window + first, count)],
            row_send.at[kind, k, j],
            row_recv.at[kind, k, j],
            peer,
        )

    table_v[2 + r] = sent[0, 0]
    halos = [
        remote(taps.at[f, 64], taps.at[f, 65], halo_send.at[f], halo_recv.at[f], (t, other))
        for f in range(2)
    ]
    tables = []
    for i, peer in enumerate(peers):
        window = (4, 0, 2, 4, 0)[i] + r
        tables.append(remote(table_v.at[2 + r], table_v.at[window], table_send.at[i], table_recv.at[i], peer))

    def send(k, j):
        for kind in range(3):
            row_copy(kind, k, j).start()

    for f in range(2):
        base = 6 * f
        split_group(f, 3)
        conv_rows(f, 31, 1)
        conv_rows(f, 29, 2)
        if f == 0:
            pl.semaphore_wait(barrier, 5)
        send(0, base)
        halos[f].start()
        conv_pairs(f, 25, 2)
        send(0, base + 1)
        for n, g in enumerate((2, 1, 0)):
            split_group(f, g)
            conv_pairs(f, 8 * g + 1, 4)
            send(0, base + 2 + n)
        halos[f].wait()
        above = taps[f, 65]
        taps[f, 0] = jnp.where(r == 0, jnp.zeros_like(above), above)
        conv_rows(f, 0, 1)
        send(0, base + 5)
        if f == 0:
            for copy in tables:
                copy.start()
    for k in range(1, len(PARTS)):
        for j in range(len(UNITS[k])):
            for kind in range(3):
                row_copy(kind, k, j).start()

    lane = lax.broadcasted_iota(jnp.int32, (WIDTH, WIDTH), 1)
    place = lax.broadcasted_iota(jnp.int32, (WIDTH, WIDTH), 0)
    mirror[...] = jnp.where(lane == WIDTH - 1 - place, 1.0, 0.0).astype(BF16)
    corr_k[...] = jnp.dot(lanes[...], corr_w[...], preferred_element_type=F32).astype(BF16)
    hid[33 * r] = jnp.zeros((WIDTH, 3 * HID), BF16)

    def clear(i, carry):
        packed[i] = jnp.zeros((WIDTH, 2 * WIDTH), F32)
        return carry

    lax.fori_loop(0, BAND, clear, 0)

    def clear_rim(i, carry):
        g1_t[i % 2 * 24 + 20 * r + i // 2] = jnp.zeros((CH, WIDTH), BF16)
        return carry

    lax.fori_loop(0, 8, clear_rim, 0)
    mid_load.wait()
    for tap in range(9):
        mid_k[tap * HID : (tap + 1) * HID, :] = mid_in[tap].T

    for copy in tables:
        copy.wait()
    to_scalar = pltpu.make_async_copy(table_v, table_s, local_sem.at[1])
    to_scalar.start()
    to_scalar.wait()

    def look_up(j, carry):
        for i in range(2):
            slot = slots[0, 0, i, j]
            window = slot // BAND
            row = table_s[window, window // 2, r, slot % BAND]
            row_of[i, j] = 2 * BAND * window + jnp.minimum(row, 2 * BAND - 1)
            weight_of[i, j] = jnp.where(row < 2 * BAND, blend[0, 0, i, j], 0.0)
        return carry

    lax.fori_loop(0, 2 * BAND, look_up, 0, unroll=4)

    lane8 = lax.broadcasted_iota(jnp.int32, (8, WIDTH), 1)
    place8 = lax.broadcasted_iota(jnp.int32, (8, WIDTH), 0)

    def forward(k):
        for j in range(len(UNITS[k])):
            for kind in range(2):
                row_copy(kind, k, j).wait_recv()
                row_copy(3 + kind, k, j).start()

    def do_part(k):
        (a0, a1), (c0, c1), (m0, m1) = PARTS[k]
        width = c1 - c0

        forward(k)
        for j in range(len(UNITS[k])):
            for kind in (2, 3, 4):
                row_copy(kind, k, j).wait_recv()

        def source(j, i):
            return weight_of[i, j] * rows[k][row_of[i, j]].astype(F32)

        def turn(where, value):
            turned = lax.dot_general(value, mirror[a0:a1], TN, preferred_element_type=F32).astype(BF16)
            if k:
                turned = g1_t[where] + turned
            g1_t[where] = turned

        def ground(i, carry):
            y = lax.rem(24 * other + i, BAND)
            parity, half = lax.rem(y, 2), y // 2
            g0[16 * parity + half, a0:a1] = (source(y, 0) + source(y, 1)).astype(BF16)
            second = (source(BAND + y, 0) + source(BAND + y, 1)).astype(BF16)
            g1[y, a0:a1] = second
            turn(24 * parity + 4 + half, second)
            return carry

        lax.fori_loop(0, 8, ground, 0, unroll=4)
        edge = remote(
            g1.at[pl.ds(24 * other, 8), pl.ds(a0, a1 - a0)],
            halo.at[:, pl.ds(a0, a1 - a0)],
            edge_send.at[0, k],
            edge_recv.at[0, k],
            (t, other),
        )
        edge.start()
        lax.fori_loop(8, BAND, ground, 0, unroll=4)
        edge.wait()

        def ground_halo(i, carry):
            turn(24 * lax.rem(i, 2) + 20 * other + i // 2, halo[i, a0:a1])
            return carry

        lax.fori_loop(0, 8, ground_halo, 0, unroll=8)

        def correlate(b, carry):
            parity, block = lax.rem(b, 2), b // 2
            first = 16 * parity + 4 * block
            second = 24 * parity + 4 * block
            for j in range(0, 12, 2):
                low, high = max(0, j - 8), min(4, j + 2)
                left_side = g0[pl.ds(first + low, high - low), c0:c1].reshape((high - low) * width, CH)
                pair = jnp.concatenate([g1_t[second + j], g1_t[second + j + 1]], axis=1)
                found = jnp.dot(left_side, pair, preferred_element_type=F32)
                for h in range(low, high):
                    for e in range(2):
                        u = j + e - h
                        if not 0 <= u < SPAN:
                            continue
                        centre = centre_of(u)
                        for x in range(c0, c1, 8):
                            at = (h - low) * width + x - c0
                            turned = pltpu.roll(
                                found[at : at + 8, e * WIDTH : (e + 1) * WIDTH],
                                (centre + 1 + x) % WIDTH,
                                1,
                                stride=1,
                                stride_axis=0,
                            )
                            mask = (lane8 >= centre - 8) & (lane8 <= centre + 8)
                            if x == 0:
                                mask = mask & (place8 + centre - lane8 >= 0)
                            if x == WIDTH - 8:
                                mask = mask & (place8 + centre - lane8 < 8)
                            pltpu.store(
                                packed.at[
                                    first + h, pl.ds(x, 8), pl.ds(WIDTH * (u // 5), WIDTH)
                                ],
                                turned,
                                mask=mask,
                            )
            return carry

        lax.fori_loop(0, 8, correlate, 0, unroll=4 if k else 1)

        kept = 16 if k else 0
        side = lax.broadcasted_iota(jnp.int32, (width + kept, HID), 0)

        def hidden(q, carry):
            scaled = (packed[pl.ds(4 * q, 4), c0:c1] * CH**-0.5).astype(BF16).reshape(4 * width, 2 * WIDTH)
            found = jnp.dot(scaled, corr_k[...], preferred_element_type=F32)
            found = jnp.maximum(found + corr_b[...], 0.0)
            for n in range(4):
                i = 4 * q + n
                at = 2 * lax.rem(i, 16) + i // 16 + 1
                value = found[n * width : (n + 1) * width]
                whole = jnp.concatenate([tail[i], value], axis=0) if k else value
                before = pltpu.roll(whole, 1, 0)
                after = pltpu.roll(whole, width + kept - 1, 0)
                if k == 0:
                    before = jnp.where(side == 0, 0.0, before)
                if k == len(PARTS) - 1:
                    after = jnp.where(side == width + kept - 1, 0.0, after)
                else:
                    tail[i] = value[width - 16 :]
                hid[at, c0:c1, 0:HID] = before[kept:].astype(BF16)
                hid[at, c0:c1, HID : 2 * HID] = value.astype(BF16)
                hid[at, m0:m1, 2 * HID : 3 * HID] = after[0 : m1 - m0].astype(BF16)
            return carry

        lax.fori_loop(0, BAND // 4, hidden, 0, unroll=2)

        rim = remote(
            hid.at[32 - 31 * r, pl.ds(m0, m1 - m0)],
            hid.at[33 * r, pl.ds(m0, m1 - m0)],
            edge_send.at[1, k],
            edge_recv.at[1, k],
            (t, other),
        )
        rim_in = remote(
            hid.at[32 - 31 * r, pl.ds(m0, m1 - m0)],
            hid.at[33 * other, pl.ds(m0, m1 - m0)],
            edge_send.at[1, k],
            edge_recv.at[1, k],
            (t, other),
        )
        rim.start()
        columns = m1 - m0

        def head(i, carry):
            y = 8 * lax.rem(i + r, 4)
            part = jnp.concatenate(
                [hid[pl.ds(y + a, 8), m0:m1].reshape(8 * columns, 3 * HID) for a in range(3)], axis=1
            )
            total = jnp.dot(part, mid_k[...], preferred_element_type=F32)
            middle = jnp.maximum(total + mid_b[...], 0.0).astype(BF16)
            flow = lax.dot_general(flow_w[...], middle, NT, preferred_element_type=F32)
            for c in range(2):
                for n in range(8):
                    out[0, c, pl.ds(y + n, 1), m0:m1] = (
                        flow[c : c + 1, n * columns : (n + 1) * columns] + flow_b[c]
                    )
            return carry

        lax.fori_loop(0, 3, head, 0)
        rim.wait_send()
        rim_in.wait_recv()
        head(3, 0)

    for k in range(len(PARTS)):
        do_part(k)

    for k in range(len(PARTS)):
        for j in range(len(UNITS[k])):
            for kind in range(5):
                row_copy(kind, k, j).wait_send()


def on_device(
    tiles,
    frames,
    feat_weight,
    feat_bias,
    send_rows,
    recv_slots,
    blend,
    corr_weight,
    corr_bias,
    mid_weight,
    mid_bias,
    flow_weight,
    flow_bias,
):
    vmem = pl.BlockSpec(memory_space=pltpu.VMEM)
    smem = pl.BlockSpec(memory_space=pltpu.SMEM)
    hbm = pl.BlockSpec(memory_space=pl.ANY)
    dma = pltpu.SemaphoreType.DMA
    parts = len(PARTS)
    return pl.pallas_call(
        functools.partial(kernel, tiles),
        out_shape=jax.ShapeDtypeStruct((1, 2, BAND, WIDTH), F32),
        in_specs=[hbm, vmem, vmem, vmem, smem, smem, vmem, vmem, vmem, hbm, vmem, vmem, smem],
        out_specs=vmem,
        scratch_shapes=[
            pltpu.VMEM((2, 4, CIN, 16, 2 * WIDTH), BF16),
            pltpu.VMEM((2 * WIDTH, 3 * WIDTH), BF16),
            pltpu.VMEM((CH, 9 * CIN), BF16),
            pltpu.VMEM((3, 16 * CIN, WIDTH), F32),
            pltpu.VMEM((2, 66, 3 * CIN, WIDTH), BF16),
            pltpu.VMEM((CH, CH), F32),
            *[pltpu.VMEM((12 * BAND, high - low, CH), BF16) for (low, high), _, _ in PARTS],
            pltpu.VMEM((6, 3, 2, BAND), jnp.int32),
            pltpu.SMEM((6, 3, 2, BAND), jnp.int32),
            pltpu.SMEM((2, 2 * BAND), jnp.int32),
            pltpu.SMEM((2, 2 * BAND), F32),
            pltpu.VMEM((BAND, WIDTH, CH), BF16),
            pltpu.VMEM((BAND, WIDTH, CH), BF16),
            pltpu.VMEM((BAND + 16, CH, WIDTH), BF16),
            pltpu.VMEM((8, WIDTH, CH), BF16),
            pltpu.VMEM((WIDTH, WIDTH), BF16),
            pltpu.VMEM((BAND, WIDTH, 2 * WIDTH), F32),
            pltpu.VMEM((2 * WIDTH, HID), BF16),
            pltpu.VMEM((BAND, 16, HID), F32),
            pltpu.VMEM((BAND + 2, WIDTH, 3 * HID), BF16),
            pltpu.VMEM((9, MID, HID), BF16),
            pltpu.VMEM((9 * HID, MID), BF16),
            dma((8,)),
            dma((2,)),
            dma((2,)),
            dma((5, parts, MOST)),
            dma((5, parts, MOST)),
            dma((5,)),
            dma((5,)),
            dma((2, parts)),
            dma((2, parts)),
            dma((2,)),
        ],
        compiler_params=pltpu.CompilerParams(
            collective_id=0, has_side_effects=True, vmem_limit_bytes=60 * 1024 * 1024
        ),
    )(
        frames,
        feat_weight.transpose(0, 2, 1).reshape(9 * CIN, CH),
        feat_bias.reshape(1, CH),
        send_rows,
        recv_slots.transpose(0, 1, 3, 2),
        blend.transpose(0, 1, 3, 2),
        jnp.asarray(offset_lanes(), BF16),
        corr_weight.T,
        corr_bias.reshape(1, HID),
        mid_weight,
        mid_bias.reshape(1, MID),
        flow_weight,
        flow_bias,
    )


def solution(mesh):
    return jax.shard_map(
        functools.partial(on_device, mesh.shape["tiles"]),
        mesh=mesh,
        in_specs=(
            P("tiles", None, None, "rows", None),
            P(),
            P(),
            P("tiles", "rows", None, None, None),
            P("tiles", "rows", None, None),
            P("tiles", "rows", None, None),
            P(),
            P(),
            P(),
            P(),
            P(),
            P(),
        ),
        out_specs=P("tiles", None, "rows", None),
        check_vma=False,
    )
```
